512 devices in a mesh: lon: 8 (over y, core), lat: 16 (over z), depth: 4 (over x).
Axes of the slice: x: 4, y: 4, z: 16, core: 2. Of those that a mesh axis runs over, the one named last changes fastest.
Arguments:
- snapshots: float32 [524288, 256], P(('lon', 'lat', 'depth')), may hold values from -300 to 300
- live_rows: int32 [512], P(('lon', 'lat', 'depth')), may hold values from 128 to 1024, as said below
- column_order: int32 [256], replicated, may hold values from 0 to 255, each once
Outputs:
- snapshot_basis: float32 [524288, 256], P(('lon', 'lat', 'depth'))
- triangular: float32 [256, 256], replicated
- highpass: float32 [524288, 256], P(('lon', 'lat', 'depth'))
The draws below stay inside these ranges and needn't reach their ends.
Inputs may be any that keep to these rules, and one draw needn't show every extreme that they name: `live_rows`: each entry is a multiple of 128; some block has all 1024 rows live and some other block has 128.
All inputs are finite; a program needn't handle non-finite values.
Results may differ from the reference program's by a relative error of at most 0.00005.
Values sent between devices are 32-bit elements; how exact they have to be, the bound alone decides.
A program may use at most 64 MiB of HBM per device.

```python
import jax
import jax.numpy as jnp
from jax import lax

S = 256
LOW = 32
ROWS_DEV = 1024
BLOCKS = 512
NROWS = 524288


def draw_snapshots(key, part):
    first = jax.random.fold_in(jax.random.fold_in(key, 11), 0)
    second = jax.random.fold_in(jax.random.fold_in(key, 11), 1)
    fourth = jax.random.fold_in(jax.random.fold_in(key, 11), 3)
    column_scale = jnp.exp(jax.random.uniform(first, (S,), jnp.float32, 0.0, 2.302585))
    block_index = (jnp.arange(NROWS, dtype=jnp.int32) // ROWS_DEV).astype(jnp.float32)
    ramp = block_index / (BLOCKS - 1)
    row_jitter = jax.random.uniform(fourth, (NROWS,), jnp.float32, 0.6, 1.4)
    values = jnp.clip(jax.random.normal(second, (NROWS, S), jnp.float32), -5.0, 5.0)
    row_scale = jnp.exp(ramp * 1.098612) * row_jitter
    result = values * column_scale[None, :] * row_scale[:, None]
    return jnp.clip(result, -300.0, 300.0).astype(jnp.float32)


def draw_live_rows(key, part):
    first, second, third = jax.random.split(jax.random.fold_in(key, 23), 3)
    counts = 128 * jax.random.randint(first, (BLOCKS,), 1, ROWS_DEV // 128 + 1)
    full_block = jax.random.randint(second, (), 0, BLOCKS)
    small_block = (full_block + 1 + jax.random.randint(third, (), 0, BLOCKS - 1)) % BLOCKS
    position = jnp.arange(BLOCKS, dtype=jnp.int32)
    counts = jnp.where(position == full_block, ROWS_DEV, counts)
    counts = jnp.where(position == small_block, 128, counts)
    return counts.astype(jnp.int32)


def setup_inputs(seed: int = 0) -> dict:
    seeds = jax.random.split(jax.random.key(seed), 4)
    return {
        "snapshots": draw_snapshots(jax.random.fold_in(seeds[3], 71), 0),
        "live_rows": draw_live_rows(jax.random.fold_in(seeds[3], 71), 0),
        "column_order": jax.random.permutation(seeds[2], S).astype(jnp.int32),
    }


def reference(snapshots, live_rows, column_order):
    picked = jnp.take(snapshots, column_order, axis=1)
    blocks = picked.reshape(-1, ROWS_DEV, S)
    live_mask = jnp.arange(ROWS_DEV, dtype=jnp.int32)[None, :] < live_rows[:, None]
    masked = jnp.where(live_mask[:, :, None], blocks, jnp.zeros_like(blocks)).reshape(-1, S)
    global_gram = lax.dot_general(masked, masked, (((0,), (0,)), ((), ())), precision=lax.Precision.HIGHEST) / NROWS
    lower_factor = jnp.linalg.cholesky(global_gram)
    triangular = lower_factor.T
    snapshot_basis = jax.scipy.linalg.solve_triangular(lower_factor, masked.T, lower=True).T
    highpass = masked - jnp.dot(snapshot_basis[:, :LOW], triangular[:LOW, :], precision=lax.Precision.HIGHEST)
    return (snapshot_basis, triangular, highpass)
```

```python
import functools

import jax
import jax.numpy as jnp
from jax import lax
from jax.experimental import pallas as pl
from jax.experimental.pallas import tpu as pltpu
from jax.sharding import PartitionSpec as P

LOW = 32
CORES = 2
HIGHEST = lax.Precision.HIGHEST


def gram_kernel(total_rows, ny, nz, nx, snap_hbm, live_ref, order_ref, masked_ref, out_ref,
                snap, gram, half, from_core, from_y, quarter, from_x, strip, from_z,
                load_sem, send_sem, recv_sem):
    rows, width = snap.shape
    lon = lax.axis_index("lon")
    core, y = lax.rem(lon, CORES), lax.div(lon, CORES)
    z, x = lax.axis_index("lat"), lax.axis_index("depth")

    def at_core(c):
        return {"lon": y * CORES + c}

    def at_y(t):
        return {"lon": t * CORES + core}

    def at_z(t):
        return {"lat": t}

    def at_x(t):
        return {"depth": t}

    peers = [at_core(1 - core)]
    for d in range(1, ny):
        peers.append(at_y(lax.rem(y + d, ny)))
    for d in range(1, nx):
        peers.append(at_x(lax.rem(x + d, nx)))
    for d in range(1, nz):
        peers.append(at_z(lax.rem(z + d, nz)))

    barrier = pltpu.get_barrier_semaphore()
    for peer in peers:
        pl.semaphore_signal(barrier, inc=1, device_id=peer, device_id_type=pl.DeviceIdType.MESH)

    load = pltpu.make_async_copy(snap_hbm, snap, load_sem)
    load.start()
    select = (lax.broadcasted_iota(jnp.int32, (width, width), 0) == order_ref[...]).astype(jnp.bfloat16)
    load.wait()

    live = lax.broadcasted_iota(jnp.int32, (rows, width), 0) < live_ref[0]
    whole = jnp.where(live, snap[...], 0.0)
    high = whole.astype(jnp.bfloat16)
    rest = whole - high.astype(jnp.float32)
    middle = rest.astype(jnp.bfloat16)
    low = (rest - middle.astype(jnp.float32)).astype(jnp.bfloat16)
    masked = jnp.dot(high, select, preferred_element_type=jnp.float32)
    masked += jnp.dot(middle, select, preferred_element_type=jnp.float32)
    masked += jnp.dot(low, select, preferred_element_type=jnp.float32)
    masked_ref[...] = masked
    gram[...] = lax.dot_general(
        masked, masked, (((0,), (0,)), ((), ())), precision=HIGHEST, preferred_element_type=jnp.float32
    ) * (1.0 / total_rows)

    pl.semaphore_wait(barrier, len(peers))

    used = [0]

    def send(src, dst, peer):
        k = used[0]
        used[0] += 1
        copy = pltpu.make_async_remote_copy(
            src_ref=src, dst_ref=dst, send_sem=send_sem.at[k], recv_sem=recv_sem.at[k],
            device_id=peer, device_id_type=pl.DeviceIdType.MESH,
        )
        copy.start()
        return copy

    def part(ref, index, size):
        return ref.at[pl.ds(pl.multiple_of(index * size, size), size)]

    n_half = width // CORES
    n_quarter = n_half // ny
    n_strip = n_quarter // nx

    copy = send(part(gram, 1 - core, n_half), from_core, at_core(1 - core))
    copy.wait()
    half[...] = gram[pl.ds(pl.multiple_of(core * n_half, n_half), n_half), :] + from_core[...]

    def scatter(src, size, slots, n, me, at):
        copies = []
        for d in range(1, n):
            t = lax.rem(me + d, n)
            copies.append(send(part(src, t, size), slots.at[me], at(t)))
        slots[me] = src[pl.ds(pl.multiple_of(me * size, size), size), :]
        for copy in copies:
            copy.wait()
        total = slots[0]
        for s in range(1, n):
            total = total + slots[s]
        return total

    quarter[...] = scatter(half, n_quarter, from_y, ny, y, at_y)
    strip[...] = scatter(quarter, n_strip, from_x, nx, x, at_x)

    copies = []
    for d in range(1, nz):
        copies.append(send(strip, from_z.at[z], at_z(lax.rem(z + d, nz))))
    from_z[z] = strip[...]
    for copy in copies:
        copy.wait()
    total = from_z[0]
    for s in range(1, nz):
        total = total + from_z[s]
    place = core * (ny * nx) + y * nx + x
    out_ref[pl.ds(pl.multiple_of(place * n_strip, n_strip), n_strip), :] = total

    def gather(index, size, n, me, at):
        copies = []
        for d in range(1, n):
            copies.append(send(part(out_ref, index, size), part(out_ref, index, size), at(lax.rem(me + d, n))))
        for copy in copies:
            copy.wait()

    gather(place, n_strip, nx, x, at_x)
    gather(core * ny + y, n_quarter, ny, y, at_y)
    gather(core, n_half, CORES, core, at_core)


def masked_and_gram(snapshots, live_rows, column_order, sizes):
    rows, width = snapshots.shape
    ny, nz, nx = sizes
    n_half = width // CORES
    n_quarter = n_half // ny
    n_strip = n_quarter // nx
    copies = 2 + 2 * (ny - 1) + 2 * (nx - 1) + (nz - 1)
    total_rows = rows * CORES * ny * nz * nx
    f32 = jnp.float32
    return pl.pallas_call(
        functools.partial(gram_kernel, total_rows, ny, nz, nx),
        out_shape=(
            jax.ShapeDtypeStruct((rows, width), f32),
            jax.ShapeDtypeStruct((width, width), f32),
        ),
        in_specs=[
            pl.BlockSpec(memory_space=pl.ANY),
            pl.BlockSpec(memory_space=pltpu.SMEM),
            pl.BlockSpec(memory_space=pltpu.VMEM),
        ],
        out_specs=(pl.BlockSpec(memory_space=pltpu.VMEM), pl.BlockSpec(memory_space=pltpu.VMEM)),
        scratch_shapes=[
            pltpu.VMEM((rows, width), f32),
            pltpu.VMEM((width, width), f32),
            pltpu.VMEM((n_half, width), f32),
            pltpu.VMEM((n_half, width), f32),
            pltpu.VMEM((ny, n_quarter, width), f32),
            pltpu.VMEM((n_quarter, width), f32),
            pltpu.VMEM((nx, n_strip, width), f32),
            pltpu.VMEM((n_strip, width), f32),
            pltpu.VMEM((nz, n_strip, width), f32),
            pltpu.SemaphoreType.DMA,
            pltpu.SemaphoreType.DMA((copies,)),
            pltpu.SemaphoreType.DMA((copies,)),
        ],
        compiler_params=pltpu.CompilerParams(collective_id=0, has_side_effects=True),
        name="gram_allreduce",
    )(snapshots, live_rows, column_order.reshape(1, width))


def on_device(sizes, snapshots, live_rows, column_order):
    masked, global_gram = masked_and_gram(snapshots, live_rows, column_order, sizes)
    lower_factor = jnp.linalg.cholesky(global_gram)
    triangular = lower_factor.T
    snapshot_basis = jax.scipy.linalg.solve_triangular(lower_factor, masked.T, lower=True).T
    highpass = masked - jnp.dot(
        snapshot_basis[:, :LOW], triangular[:LOW, :], precision=lax.Precision.HIGHEST
    )
    return (snapshot_basis, triangular, highpass)


def solution(mesh):
    placed = (P(("lon", "lat", "depth"), None), P(("lon", "lat", "depth")), P())
    sizes = (mesh.shape["lon"] // CORES, mesh.shape["lat"], mesh.shape["depth"])
    return jax.shard_map(
        functools.partial(on_device, sizes),
        mesh=mesh,
        in_specs=placed,
        out_specs=(P(("lon", "lat", "depth"), None), P(), P(("lon", "lat", "depth"), None)),
        check_vma=False,
    )
```

```python
import functools

import jax
import jax.numpy as jnp
from jax import lax
from jax.experimental import pallas as pl
from jax.experimental.pallas import tpu as pltpu
from jax.sharding import PartitionSpec as P

LOW = 32
CORES = 2
LANES = 128
TILE = 8
HIGHEST = lax.Precision.HIGHEST


def gram_kernel(total_rows, ny, nz, nx, snap_hbm, live_ref, order_ref, masked_ref, out_ref,
                snap, gram, half, from_core, from_y, quarter, from_x, strip, from_z,
                load_sem, send_sem, recv_sem):
    rows, width = snap.shape
    lon = lax.axis_index("lon")
    core, y = lax.rem(lon, CORES), lax.div(lon, CORES)
    z, x = lax.axis_index("lat"), lax.axis_index("depth")

    def at_core(c):
        return {"lon": y * CORES + c}

    def at_y(t):
        return {"lon": t * CORES + core}

    def at_z(t):
        return {"lat": t}

    def at_x(t):
        return {"depth": t}

    peers = [at_core(1 - core)]
    for d in range(1, ny):
        peers.append(at_y(lax.rem(y + d, ny)))
    for d in range(1, nx):
        peers.append(at_x(lax.rem(x + d, nx)))
    for d in range(1, nz):
        peers.append(at_z(lax.rem(z + d, nz)))

    barrier = pltpu.get_barrier_semaphore()
    for peer in peers:
        pl.semaphore_signal(barrier, inc=1, device_id=peer, device_id_type=pl.DeviceIdType.MESH)

    load = pltpu.make_async_copy(snap_hbm, snap, load_sem)
    load.start()
    select = (lax.broadcasted_iota(jnp.int32, (width, width), 0) == order_ref[...]).astype(jnp.bfloat16)
    load.wait()

    live = lax.broadcasted_iota(jnp.int32, (rows, width), 0) < live_ref[0]
    whole = jnp.where(live, snap[...], 0.0)
    high = whole.astype(jnp.bfloat16)
    rest = whole - high.astype(jnp.float32)
    middle = rest.astype(jnp.bfloat16)
    low = (rest - middle.astype(jnp.float32)).astype(jnp.bfloat16)
    masked = jnp.dot(high, select, preferred_element_type=jnp.float32)
    masked += jnp.dot(middle, select, preferred_element_type=jnp.float32)
    masked += jnp.dot(low, select, preferred_element_type=jnp.float32)
    masked_ref[...] = masked
    gram[...] = lax.dot_general(
        masked, masked, (((0,), (0,)), ((), ())), precision=HIGHEST, preferred_element_type=jnp.float32
    ) * (1.0 / total_rows)

    pl.semaphore_wait(barrier, len(peers))

    used = [0]

    def send(src, dst, peer):
        k = used[0]
        used[0] += 1
        copy = pltpu.make_async_remote_copy(
            src_ref=src, dst_ref=dst, send_sem=send_sem.at[k], recv_sem=recv_sem.at[k],
            device_id=peer, device_id_type=pl.DeviceIdType.MESH,
        )
        copy.start()
        return copy

    def part(ref, index, size):
        return ref.at[pl.ds(pl.multiple_of(index * size, size), size)]

    n_half = width // CORES
    n_quarter = n_half // ny
    n_strip = n_quarter // nx

    copy = send(part(gram, 1 - core, n_half), from_core, at_core(1 - core))
    copy.wait()
    half[...] = gram[pl.ds(pl.multiple_of(core * n_half, n_half), n_half), :] + from_core[...]

    def scatter(src, size, slots, n, me, at):
        copies = []
        for d in range(1, n):
            t = lax.rem(me + d, n)
            copies.append(send(part(src, t, size), slots.at[me], at(t)))
        slots[me] = src[pl.ds(pl.multiple_of(me * size, size), size), :]
        for copy in copies:
            copy.wait()
        total = slots[0]
        for s in range(1, n):
            total = total + slots[s]
        return total

    quarter[...] = scatter(half, n_quarter, from_y, ny, y, at_y)
    strip[...] = scatter(quarter, n_strip, from_x, nx, x, at_x)

    copies = []
    for d in range(1, nz):
        copies.append(send(strip, from_z.at[z], at_z(lax.rem(z + d, nz))))
    from_z[z] = strip[...]
    for copy in copies:
        copy.wait()
    total = from_z[0]
    for s in range(1, nz):
        total = total + from_z[s]
    place = core * (ny * nx) + y * nx + x
    out_ref[pl.ds(pl.multiple_of(place * n_strip, n_strip), n_strip), :] = total

    def gather(index, size, n, me, at):
        copies = []
        for d in range(1, n):
            copies.append(send(part(out_ref, index, size), part(out_ref, index, size), at(lax.rem(me + d, n))))
        for copy in copies:
            copy.wait()

    gather(place, n_strip, nx, x, at_x)
    gather(core * ny + y, n_quarter, ny, y, at_y)
    gather(core, n_half, CORES, core, at_core)


def masked_and_gram(snapshots, live_rows, column_order, sizes):
    rows, width = snapshots.shape
    ny, nz, nx = sizes
    n_half = width // CORES
    n_quarter = n_half // ny
    n_strip = n_quarter // nx
    copies = 2 + 2 * (ny - 1) + 2 * (nx - 1) + (nz - 1)
    total_rows = rows * CORES * ny * nz * nx
    f32 = jnp.float32
    return pl.pallas_call(
        functools.partial(gram_kernel, total_rows, ny, nz, nx),
        out_shape=(
            jax.ShapeDtypeStruct((rows, width), f32),
            jax.ShapeDtypeStruct((width, width), f32),
        ),
        in_specs=[
            pl.BlockSpec(memory_space=pl.ANY),
            pl.BlockSpec(memory_space=pltpu.SMEM),
            pl.BlockSpec(memory_space=pltpu.VMEM),
        ],
        out_specs=(pl.BlockSpec(memory_space=pltpu.VMEM), pl.BlockSpec(memory_space=pltpu.VMEM)),
        scratch_shapes=[
            pltpu.VMEM((rows, width), f32),
            pltpu.VMEM((width, width), f32),
            pltpu.VMEM((n_half, width), f32),
            pltpu.VMEM((n_half, width), f32),
            pltpu.VMEM((ny, n_quarter, width), f32),
            pltpu.VMEM((n_quarter, width), f32),
            pltpu.VMEM((nx, n_strip, width), f32),
            pltpu.VMEM((n_strip, width), f32),
            pltpu.VMEM((nz, n_strip, width), f32),
            pltpu.SemaphoreType.DMA,
            pltpu.SemaphoreType.DMA((copies,)),
            pltpu.SemaphoreType.DMA((copies,)),
        ],
        compiler_params=pltpu.CompilerParams(collective_id=0, has_side_effects=True),
        name="gram_allreduce",
    )(snapshots, live_rows, column_order.reshape(1, width))


def factor_kernel(group, gram_ref, masked_ref, basis_ref, tri_ref, high_ref, work, inverse):
    width = gram_ref.shape[0]
    rows = masked_ref.shape[0]
    blocks = width // TILE
    per_lanes = LANES // TILE
    f32 = jnp.float32
    shape = (TILE, LANES)
    sub = lax.broadcasted_iota(jnp.int32, shape, 0)
    lane = lax.broadcasted_iota(jnp.int32, shape, 1)

    def band(i):
        return slice(i * TILE, (i + 1) * TILE)

    def lanes(v):
        return slice(v * LANES, (v + 1) * LANES)

    work[...] = gram_ref[...]
    row_id = lax.broadcasted_iota(jnp.int32, (width, width), 0)
    col_id = lax.broadcasted_iota(jnp.int32, (width, width), 1)
    inverse[...] = (row_id == col_id).astype(f32)
    tri_ref[...] = jnp.zeros_like(tri_ref)

    chunk = 128

    def finish_high(c):
        here = slice(c * chunk, (c + 1) * chunk)
        a = masked_ref[here, :]
        q = lax.dot_general(a, inverse[:LOW, :], (((1,), (1,)), ((), ())), precision=HIGHEST,
                            preferred_element_type=f32)
        high_ref[here, :] = a - jnp.dot(q, tri_ref[:LOW, :], precision=HIGHEST, preferred_element_type=f32)

    def finish_basis(c, half):
        here = slice(c * chunk, (c + 1) * chunk)
        depth = (half + 1) * LANES
        basis_ref[here, lanes(half)] = lax.dot_general(
            masked_ref[here, :depth], inverse[lanes(half), :depth], (((1,), (1,)), ((), ())),
            precision=HIGHEST, preferred_element_type=f32)

    fillers = []

    for k in range(blocks):
        t = k // per_lanes
        base = (k % per_lanes) * TILE
        last = (k // group + 1) * group
        row = {}
        for j in range(TILE):
            r = k * TILE + j
            for v in range(t, width // LANES):
                row["g", v, j] = jnp.broadcast_to(work[r:r + 1, lanes(v)], shape)
            for v in range(0, t + 1):
                row["x", v, j] = jnp.broadcast_to(inverse[r:r + 1, lanes(v)], shape)
        items = [("g", v) for v in range(t, width // LANES)] + [("x", v) for v in range(0, t + 1)]
        a = {}
        for j in range(TILE):
            for m in range(j, TILE):
                a[j, m] = jnp.broadcast_to(row["g", t, j][:, base + m:base + m + 1], shape)
        col = {}
        for i in range(k + 1, last):
            tile = work[band(i), lanes(t)]
            for j in range(TILE):
                col[i, j] = jnp.broadcast_to(tile[:, base + j:base + j + 1], shape)
        for j in range(TILE):
            s = lax.rsqrt(a[j, j])
            for m in range(j + 1, TILE):
                a[j, m] = a[j, m] * s
            for m in range(j + 1, TILE):
                for p in range(m, TILE):
                    a[m, p] = a[m, p] - a[j, m] * a[j, p]
            for i in range(k + 1, last):
                col[i, j] = col[i, j] * s
                for m in range(j + 1, TILE):
                    col[i, m] = col[i, m] - a[j, m] * col[i, j]
            for kind, v in items:
                row[kind, v, j] = row[kind, v, j] * s
                for m in range(j + 1, TILE):
                    row[kind, v, m] = row[kind, v, m] - a[j, m] * row[kind, v, j]
        for i in range(k + 1, last):
            for kind, v in items:
                ref = work if kind == "g" else inverse
                change = [col[i, j] * row[kind, v, j] for j in range(TILE)]
                while len(change) > 1:
                    change = [p + q for p, q in zip(change[::2], change[1::2])]
                ref[band(i), lanes(v)] = ref[band(i), lanes(v)] - change[0]
        for kind, v in items:
            tile = row[kind, v, TILE - 1]
            for j in range(TILE - 2, -1, -1):
                tile = jnp.where(sub == j, row[kind, v, j], tile)
            if kind == "g":
                if v == t:
                    tile = jnp.where(lane >= sub + base, tile, 0.0)
                tri_ref[band(k), lanes(v)] = tile
            else:
                inverse[band(k), lanes(v)] = tile

        if k + 1 == last and last < blocks:
            first = last - group
            done = slice(first * TILE, last * TILE)
            low = (last // per_lanes) * LANES
            span = (t + 1) * LANES
            left = tri_ref[done, low:]
            dims = (((0,), (0,)), ((), ()))
            drop = lax.dot_general(left, tri_ref[done, low:], dims, precision=HIGHEST, preferred_element_type=f32)
            fill = lax.dot_general(left, inverse[done, :span], dims, precision=HIGHEST, preferred_element_type=f32)
            skip = last * TILE - low
            work[last * TILE:, low:] = work[last * TILE:, low:] - drop[skip:, :]
            inverse[last * TILE:, :span] = inverse[last * TILE:, :span] - fill[skip:, :]
        if (k + 1) * TILE == LOW:
            fillers += [functools.partial(finish_high, c) for c in range(rows // chunk)]
        if (k + 1) * TILE == LANES:
            fillers += [functools.partial(finish_basis, c, 0) for c in range(rows // chunk)]
        if fillers:
            fillers.pop(0)()
    for c in range(rows // chunk):
        fillers.append(functools.partial(finish_basis, c, 1))
    for filler in fillers:
        filler()


def factor(gram, masked, group=4):
    rows, width = masked.shape
    f32 = jnp.float32
    vmem = pl.BlockSpec(memory_space=pltpu.VMEM)
    return pl.pallas_call(
        functools.partial(factor_kernel, group),
        out_shape=(
            jax.ShapeDtypeStruct((rows, width), f32),
            jax.ShapeDtypeStruct((width, width), f32),
            jax.ShapeDtypeStruct((rows, width), f32),
        ),
        in_specs=[vmem, vmem],
        out_specs=(vmem, vmem, vmem),
        scratch_shapes=[pltpu.VMEM((width, width), f32), pltpu.VMEM((width, width), f32)],
        name="factor",
    )(gram, masked)


def on_device(sizes, snapshots, live_rows, column_order):
    masked, global_gram = masked_and_gram(snapshots, live_rows, column_order, sizes)
    return factor(global_gram, masked)


def solution(mesh):
    placed = (P(("lon", "lat", "depth"), None), P(("lon", "lat", "depth")), P())
    sizes = (mesh.shape["lon"] // CORES, mesh.shape["lat"], mesh.shape["depth"])
    return jax.shard_map(
        functools.partial(on_device, sizes),
        mesh=mesh,
        in_specs=placed,
        out_specs=(P(("lon", "lat", "depth"), None), P(), P(("lon", "lat", "depth"), None)),
        check_vma=False,
    )
```

```python
import functools

import jax
import jax.numpy as jnp
from jax import lax
from jax.experimental import pallas as pl
from jax.experimental.pallas import tpu as pltpu
from jax.sharding import PartitionSpec as P

LOW = 32
CORES = 2
LANES = 128
TILE = 8
UNIT = 4
HIGHEST = lax.Precision.HIGHEST


def hops(d, n):
    return min(d % n, n - d % n)


def gram_kernel(total_rows, ny, nz, nx, snap_hbm, live_ref, order_ref, masked_hbm, out_ref,
                snap, masked_ref, gram, from_core, half, from_plane, strip, from_z,
                load_sem, store_sem, send_sem, recv_sem):
    rows, width = snap.shape
    lon = lax.axis_index("lon")
    core, y = lax.rem(lon, CORES), lax.div(lon, CORES)
    z, x = lax.axis_index("lat"), lax.axis_index("depth")
    f32 = jnp.float32

    plane = [(dy, dx) for dy in range(ny) for dx in range(nx) if dy or dx]
    plane.sort(key=lambda d: -hops(d[0], ny) - hops(d[1], nx))
    line = sorted(range(1, nz), key=lambda d: -hops(d, nz))

    def other_core():
        return {"lon": y * CORES + 1 - core}

    def in_plane(dy, dx):
        return lax.rem(y + dy, ny), lax.rem(x + dx, nx)

    def at_plane(dy, dx):
        ty, tx = in_plane(dy, dx)
        return {"lon": ty * CORES + core, "depth": tx}

    def at_z(d):
        return {"lat": lax.rem(z + d, nz)}

    peers = [at_z(d) for d in line] + [at_plane(*d) for d in plane] + [other_core()]
    barrier = pltpu.get_barrier_semaphore()
    for peer in peers:
        pl.semaphore_signal(barrier, inc=1, device_id=peer, device_id_type=pl.DeviceIdType.MESH)

    load = pltpu.make_async_copy(snap_hbm, snap, load_sem)
    load.start()
    select = (lax.broadcasted_iota(jnp.int32, (width, width), 0) == order_ref[...]).astype(jnp.bfloat16)
    load.wait()

    live = lax.broadcasted_iota(jnp.int32, (rows, width), 0) < live_ref[0]
    whole = jnp.where(live, snap[...], 0.0)
    high = whole.astype(jnp.bfloat16)
    rest = whole - high.astype(f32)
    middle = rest.astype(jnp.bfloat16)
    low = (rest - middle.astype(f32)).astype(jnp.bfloat16)
    masked = jnp.dot(high, select, preferred_element_type=f32)
    masked += jnp.dot(middle, select, preferred_element_type=f32)
    masked += jnp.dot(low, select, preferred_element_type=f32)
    masked_ref[...] = masked
    store = pltpu.make_async_copy(masked_ref, masked_hbm, store_sem)
    store.start()

    left, right = masked[:, :LANES], masked[:, LANES:]

    def product(a, b, at):
        block = lax.dot_general(a, b, (((0,), (0,)), ((), ())), precision=HIGHEST, preferred_element_type=f32)
        gram[at * LANES // UNIT:(at + 1) * LANES // UNIT] = (block * (1.0 / total_rows)).reshape(
            LANES // UNIT, UNIT, LANES)

    product(left, left, 0)
    product(left, right, 1)
    product(right, right, 2)

    pl.semaphore_wait(barrier, len(peers))

    used = [0]

    def send(src, dst, peer):
        k = used[0]
        used[0] += 1
        copy = pltpu.make_async_remote_copy(
            src_ref=src, dst_ref=dst, send_sem=send_sem.at[k], recv_sem=recv_sem.at[k],
            device_id=peer, device_id_type=pl.DeviceIdType.MESH,
        )
        copy.start()
        return copy

    places = ny * nx
    n_half = half.shape[0]
    n_strip = n_half // places
    place = y * nx + x

    copy = send(gram.at[pl.ds((1 - core) * n_half, n_half)], from_core, other_core())
    copy.wait()
    half[...] = gram[pl.ds(core * n_half, n_half)] + from_core[...]

    copies = []
    for d in plane:
        ty, tx = in_plane(*d)
        copies.append(send(half.at[pl.ds((ty * nx + tx) * n_strip, n_strip)], from_plane.at[place], at_plane(*d)))
    from_plane[place] = half[pl.ds(place * n_strip, n_strip)]
    for copy in copies:
        copy.wait()
    total = from_plane[0]
    for s in range(1, places):
        total = total + from_plane[s]
    strip[...] = total

    copies = [send(strip, from_z.at[z], at_z(d)) for d in line]
    from_z[z] = strip[...]
    for copy in copies:
        copy.wait()
    total = from_z[0]
    for s in range(1, nz):
        total = total + from_z[s]
    mine = pl.ds((core * places + place) * n_strip, n_strip)
    out_ref[mine] = total

    copies = [send(out_ref.at[mine], out_ref.at[mine], at_plane(*d)) for d in plane]
    for copy in copies:
        copy.wait()
    mine = pl.ds(core * n_half, n_half)
    copy = send(out_ref.at[mine], out_ref.at[mine], other_core())
    copy.wait()
    store.wait()


def masked_and_gram(snapshots, live_rows, column_order, sizes):
    rows, width = snapshots.shape
    ny, nz, nx = sizes
    places = ny * nx
    units = 3 * LANES // UNIT
    n_half = units // CORES
    n_strip = n_half // places
    copies = 2 + 2 * (places - 1) + (nz - 1)
    total_rows = rows * CORES * places * nz
    f32 = jnp.float32
    tile = (UNIT, LANES)
    masked, gram = pl.pallas_call(
        functools.partial(gram_kernel, total_rows, ny, nz, nx),
        out_shape=(
            jax.ShapeDtypeStruct((rows, width), f32),
            jax.ShapeDtypeStruct((units, *tile), f32),
        ),
        in_specs=[
            pl.BlockSpec(memory_space=pl.ANY),
            pl.BlockSpec(memory_space=pltpu.SMEM),
            pl.BlockSpec(memory_space=pltpu.VMEM),
        ],
        out_specs=(pl.BlockSpec(memory_space=pl.ANY), pl.BlockSpec(memory_space=pltpu.VMEM)),
        scratch_shapes=[
            pltpu.VMEM((rows, width), f32),
            pltpu.VMEM((rows, width), f32),
            pltpu.VMEM((units, *tile), f32),
            pltpu.VMEM((n_half, *tile), f32),
            pltpu.VMEM((n_half, *tile), f32),
            pltpu.VMEM((places, n_strip, *tile), f32),
            pltpu.VMEM((n_strip, *tile), f32),
            pltpu.VMEM((nz, n_strip, *tile), f32),
            pltpu.SemaphoreType.DMA,
            pltpu.SemaphoreType.DMA,
            pltpu.SemaphoreType.DMA((copies,)),
            pltpu.SemaphoreType.DMA((copies,)),
        ],
        compiler_params=pltpu.CompilerParams(collective_id=0, has_side_effects=True),
        name="gram_allreduce",
    )(snapshots, live_rows, column_order.reshape(1, width))
    return masked, gram.reshape(3 * LANES, LANES)


def factor_kernel(group, gram_ref, masked_ref, basis_ref, tri_ref, high_ref, work, inverse):
    rows, width = masked_ref.shape
    blocks = width // TILE
    per_lanes = LANES // TILE
    f32 = jnp.float32
    shape = (TILE, LANES)
    sub = lax.broadcasted_iota(jnp.int32, shape, 0)
    lane = lax.broadcasted_iota(jnp.int32, shape, 1)

    def band(i):
        return slice(i * TILE, (i + 1) * TILE)

    def lanes(v):
        return slice(v * LANES, (v + 1) * LANES)

    work[:LANES, :LANES] = gram_ref[:LANES, :]
    work[:LANES, LANES:] = gram_ref[LANES:2 * LANES, :]
    work[LANES:, :LANES] = jnp.zeros((width - LANES, LANES), f32)
    work[LANES:, LANES:] = gram_ref[2 * LANES:, :]
    row_id = lax.broadcasted_iota(jnp.int32, (width, width), 0)
    col_id = lax.broadcasted_iota(jnp.int32, (width, width), 1)
    inverse[...] = (row_id == col_id).astype(f32)
    tri_ref[...] = jnp.zeros_like(tri_ref)

    chunk = 128

    def finish_high(c):
        here = slice(c * chunk, (c + 1) * chunk)
        a = masked_ref[here, :]
        q = lax.dot_general(a, inverse[:LOW, :], (((1,), (1,)), ((), ())), precision=HIGHEST,
                            preferred_element_type=f32)
        high_ref[here, :] = a - jnp.dot(q, tri_ref[:LOW, :], precision=HIGHEST, preferred_element_type=f32)

    def finish_basis(c, half):
        here = slice(c * chunk, (c + 1) * chunk)
        depth = (half + 1) * LANES
        basis_ref[here, lanes(half)] = lax.dot_general(
            masked_ref[here, :depth], inverse[lanes(half), :depth], (((1,), (1,)), ((), ())),
            precision=HIGHEST, preferred_element_type=f32)

    fillers = []

    for k in range(blocks):
        t = k // per_lanes
        base = (k % per_lanes) * TILE
        last = (k // group + 1) * group
        row = {}
        for j in range(TILE):
            r = k * TILE + j
            for v in range(t, width // LANES):
                row["g", v, j] = jnp.broadcast_to(work[r:r + 1, lanes(v)], shape)
            for v in range(0, t + 1):
                row["x", v, j] = jnp.broadcast_to(inverse[r:r + 1, lanes(v)], shape)
        items = [("g", v) for v in range(t, width // LANES)] + [("x", v) for v in range(0, t + 1)]
        a = {}
        for j in range(TILE):
            for m in range(j, TILE):
                a[j, m] = jnp.broadcast_to(row["g", t, j][:, base + m:base + m + 1], shape)
        col = {}
        for i in range(k + 1, last):
            tile = work[band(i), lanes(t)]
            for j in range(TILE):
                col[i, j] = jnp.broadcast_to(tile[:, base + j:base + j + 1], shape)
        for j in range(TILE):
            s = lax.rsqrt(a[j, j])
            for m in range(j + 1, TILE):
                a[j, m] = a[j, m] * s
            for m in range(j + 1, TILE):
                for p in range(m, TILE):
                    a[m, p] = a[m, p] - a[j, m] * a[j, p]
            for i in range(k + 1, last):
                col[i, j] = col[i, j] * s
                for m in range(j + 1, TILE):
                    col[i, m] = col[i, m] - a[j, m] * col[i, j]
            for kind, v in items:
                row[kind, v, j] = row[kind, v, j] * s
                for m in range(j + 1, TILE):
                    row[kind, v, m] = row[kind, v, m] - a[j, m] * row[kind, v, j]
        for i in range(k + 1, last):
            for kind, v in items:
                ref = work if kind == "g" else inverse
                change = [col[i, j] * row[kind, v, j] for j in range(TILE)]
                while len(change) > 1:
                    change = [p + q for p, q in zip(change[::2], change[1::2])]
                ref[band(i), lanes(v)] = ref[band(i), lanes(v)] - change[0]
        for kind, v in items:
            tile = row[kind, v, TILE - 1]
            for j in range(TILE - 2, -1, -1):
                tile = jnp.where(sub == j, row[kind, v, j], tile)
            if kind == "g":
                if v == t:
                    tile = jnp.where(lane >= sub + base, tile, 0.0)
                tri_ref[band(k), lanes(v)] = tile
            else:
                inverse[band(k), lanes(v)] = tile

        if k + 1 == last and last < blocks:
            first = last - group
            done = slice(first * TILE, last * TILE)
            low = (last // per_lanes) * LANES
            span = (t + 1) * LANES
            left = tri_ref[done, low:]
            dims = (((0,), (0,)), ((), ()))
            drop = lax.dot_general(left, tri_ref[done, low:], dims, precision=HIGHEST, preferred_element_type=f32)
            fill = lax.dot_general(left, inverse[done, :span], dims, precision=HIGHEST, preferred_element_type=f32)
            skip = last * TILE - low
            work[last * TILE:, low:] = work[last * TILE:, low:] - drop[skip:, :]
            inverse[last * TILE:, :span] = inverse[last * TILE:, :span] - fill[skip:, :]
        if (k + 1) * TILE == LOW:
            fillers += [functools.partial(finish_high, c) for c in range(rows // chunk)]
        if (k + 1) * TILE == LANES:
            fillers += [functools.partial(finish_basis, c, 0) for c in range(rows // chunk)]
        if fillers:
            fillers.pop(0)()
    for c in range(rows // chunk):
        fillers.append(functools.partial(finish_basis, c, 1))
    for filler in fillers:
        filler()


def factor(gram, masked, group=4):
    rows, width = masked.shape
    f32 = jnp.float32
    vmem = pl.BlockSpec(memory_space=pltpu.VMEM)
    return pl.pallas_call(
        functools.partial(factor_kernel, group),
        out_shape=(
            jax.ShapeDtypeStruct((rows, width), f32),
            jax.ShapeDtypeStruct((width, width), f32),
            jax.ShapeDtypeStruct((rows, width), f32),
        ),
        in_specs=[vmem, vmem],
        out_specs=(vmem, vmem, vmem),
        scratch_shapes=[pltpu.VMEM((width, width), f32), pltpu.VMEM((width, width), f32)],
        name="factor",
    )(gram, masked)


def on_device(sizes, snapshots, live_rows, column_order):
    masked, global_gram = masked_and_gram(snapshots, live_rows, column_order, sizes)
    return factor(global_gram, masked)


def solution(mesh):
    placed = (P(("lon", "lat", "depth"), None), P(("lon", "lat", "depth")), P())
    sizes = (mesh.shape["lon"] // CORES, mesh.shape["lat"], mesh.shape["depth"])
    return jax.shard_map(
        functools.partial(on_device, sizes),
        mesh=mesh,
        in_specs=placed,
        out_specs=(P(("lon", "lat", "depth"), None), P(), P(("lon", "lat", "depth"), None)),
        check_vma=False,
    )
```

```python
import functools

import jax
import jax.numpy as jnp
from jax import lax
from jax.experimental import pallas as pl
from jax.experimental.pallas import tpu as pltpu
from jax.sharding import PartitionSpec as P

LOW = 32
CORES = 2
LANES = 128
TILE = 8
UNIT = 4
LOADS = 4
BF16 = jnp.bfloat16
TERMS = ((2, 0), (0, 2), (1, 1), (1, 0), (0, 1), (0, 0))
HIGHEST = lax.Precision.HIGHEST


def hops(d, n):
    return min(d % n, n - d % n)


def gram_kernel(total_rows, ny, nz, nx, snap_hbm, live_ref, order_ref, out_ref, high_hbm, middle_hbm, low_hbm,
                snap, high_ref, middle_ref, low_ref, gram, from_core, half, from_plane, strip, from_z,
                load_sem, store_sem, send_sem, recv_sem):
    rows, width = snap.shape
    lon = lax.axis_index("lon")
    core, y = lax.rem(lon, CORES), lax.div(lon, CORES)
    z, x = lax.axis_index("lat"), lax.axis_index("depth")
    f32 = jnp.float32
    data = (high_ref, middle_ref, low_ref)
    data_hbm = (high_hbm, middle_hbm, low_hbm)

    plane = [(dy, dx) for dy in range(ny) for dx in range(nx) if dy or dx]
    plane.sort(key=lambda d: -hops(d[0], ny) - hops(d[1], nx))
    line = sorted(range(1, nz), key=lambda d: -hops(d, nz))

    def other_core():
        return {"lon": y * CORES + 1 - core}

    def in_plane(dy, dx):
        return lax.rem(y + dy, ny), lax.rem(x + dx, nx)

    def at_plane(dy, dx):
        ty, tx = in_plane(dy, dx)
        return {"lon": ty * CORES + core, "depth": tx}

    def at_z(d):
        return {"lat": lax.rem(z + d, nz)}

    size = rows // LOADS
    loads = []
    for c in range(LOADS):
        here = pl.ds(c * size, size)
        load = pltpu.make_async_copy(snap_hbm.at[here], snap.at[here], load_sem.at[c])
        load.start()
        loads.append(load)

    peers = [at_z(d) for d in line] + [at_plane(*d) for d in plane] + [other_core()]
    barrier = pltpu.get_barrier_semaphore()
    for peer in peers:
        pl.semaphore_signal(barrier, inc=1, device_id=peer, device_id_type=pl.DeviceIdType.MESH)

    select = (lax.broadcasted_iota(jnp.int32, (width, width), 0) == order_ref[...]).astype(BF16)
    for c in range(LOADS):
        loads[c].wait()
        here = slice(c * size, (c + 1) * size)
        live = lax.broadcasted_iota(jnp.int32, (size, width), 0) + c * size < live_ref[0]
        for piece, ref in zip(pieces(jnp.where(live, snap[here, :], 0.0)), data):
            ref[here, :] = jnp.dot(piece, select, preferred_element_type=f32).astype(BF16)
    stores = []
    for p, (src, dst) in enumerate(zip(data, data_hbm)):
        store = pltpu.make_async_copy(src, dst, store_sem.at[p])
        store.start()
        stores.append(store)

    def inner(a, b):
        return lax.dot_general(a, b, (((0,), (0,)), ((), ())), preferred_element_type=f32)

    high, middle, low = (ref[...] for ref in data)
    cross = inner(high, low) + inner(high, middle)
    whole = (inner(middle, middle) + (cross + cross.T) + inner(high, high)) * (1.0 / total_rows)

    blocks = (whole[:LANES, :LANES], whole[:LANES, LANES:], whole[LANES:, LANES:])
    per_block = LANES // UNIT
    for at, block in enumerate(blocks):
        gram[at * per_block:(at + 1) * per_block] = block.reshape(per_block, UNIT, LANES)

    pl.semaphore_wait(barrier, len(peers))

    used = [0]

    def send(src, dst, peer):
        k = used[0]
        used[0] += 1
        copy = pltpu.make_async_remote_copy(
            src_ref=src, dst_ref=dst, send_sem=send_sem.at[k], recv_sem=recv_sem.at[k],
            device_id=peer, device_id_type=pl.DeviceIdType.MESH,
        )
        copy.start()
        return copy

    places = ny * nx
    n_half = half.shape[0]
    n_strip = n_half // places
    place = y * nx + x

    copy = send(gram.at[pl.ds((1 - core) * n_half, n_half)], from_core, other_core())
    copy.wait()
    half[...] = gram[pl.ds(core * n_half, n_half)] + from_core[...]

    copies = []
    for d in plane:
        ty, tx = in_plane(*d)
        copies.append(send(half.at[pl.ds((ty * nx + tx) * n_strip, n_strip)], from_plane.at[place], at_plane(*d)))
    from_plane[place] = half[pl.ds(place * n_strip, n_strip)]
    for copy in copies:
        copy.wait()
    total = from_plane[0]
    for s in range(1, places):
        total = total + from_plane[s]
    strip[...] = total

    copies = [send(strip, from_z.at[z], at_z(d)) for d in line]
    from_z[z] = strip[...]
    for copy in copies:
        copy.wait()
    total = from_z[0]
    for s in range(1, nz):
        total = total + from_z[s]
    mine = pl.ds((core * places + place) * n_strip, n_strip)
    out_ref[mine] = total

    copies = [send(out_ref.at[mine], out_ref.at[mine], at_plane(*d)) for d in plane]
    for copy in copies:
        copy.wait()
    mine = pl.ds(core * n_half, n_half)
    copy = send(out_ref.at[mine], out_ref.at[mine], other_core())
    copy.wait()
    for store in stores:
        store.wait()


def masked_and_gram(snapshots, live_rows, column_order, sizes):
    rows, width = snapshots.shape
    ny, nz, nx = sizes
    places = ny * nx
    units = 3 * LANES // UNIT
    n_half = units // CORES
    n_strip = n_half // places
    copies = 2 + 2 * (places - 1) + (nz - 1)
    total_rows = rows * CORES * places * nz
    f32 = jnp.float32
    tile = (UNIT, LANES)
    gram, *masked = pl.pallas_call(
        functools.partial(gram_kernel, total_rows, ny, nz, nx),
        out_shape=(
            jax.ShapeDtypeStruct((units, *tile), f32),
            *[jax.ShapeDtypeStruct((rows, width), BF16)] * 3,
        ),
        in_specs=[
            pl.BlockSpec(memory_space=pl.ANY),
            pl.BlockSpec(memory_space=pltpu.SMEM),
            pl.BlockSpec(memory_space=pltpu.VMEM),
        ],
        out_specs=(pl.BlockSpec(memory_space=pltpu.VMEM), *[pl.BlockSpec(memory_space=pl.ANY)] * 3),
        scratch_shapes=[
            pltpu.VMEM((rows, width), f32),
            *[pltpu.VMEM((rows, width), BF16)] * 3,
            pltpu.VMEM((units, *tile), f32),
            pltpu.VMEM((n_half, *tile), f32),
            pltpu.VMEM((n_half, *tile), f32),
            pltpu.VMEM((places, n_strip, *tile), f32),
            pltpu.VMEM((n_strip, *tile), f32),
            pltpu.VMEM((nz, n_strip, *tile), f32),
            pltpu.SemaphoreType.DMA((LOADS,)),
            pltpu.SemaphoreType.DMA((3,)),
            pltpu.SemaphoreType.DMA((copies,)),
            pltpu.SemaphoreType.DMA((copies,)),
        ],
        compiler_params=pltpu.CompilerParams(collective_id=0, has_side_effects=True),
        name="gram_allreduce",
    )(snapshots, live_rows, column_order.reshape(1, width))
    return gram.reshape(3 * LANES, LANES), *masked


def pieces(value):
    high = value.astype(BF16)
    rest = value - high.astype(jnp.float32)
    middle = rest.astype(BF16)
    return high, middle, (rest - middle.astype(jnp.float32)).astype(BF16)


def product(a, b, dims):
    out = None
    for p, q in TERMS:
        term = lax.dot_general(a[p], b[q], (dims, ((), ())), preferred_element_type=jnp.float32)
        out = term if out is None else out + term
    return out


def factor_kernel(group, chunk, tail, gram_ref, high_ref, middle_ref, low_ref, basis_ref, tri_ref, pass_ref, work, inverse, right_ref):
    rows, width = high_ref.shape
    blocks = width // TILE
    per_lanes = LANES // TILE
    f32 = jnp.float32
    shape = (TILE, LANES)
    sub = lax.broadcasted_iota(jnp.int32, shape, 0)
    lane = lax.broadcasted_iota(jnp.int32, shape, 1)
    data = (high_ref, middle_ref, low_ref)

    def band(i):
        return slice(i * TILE, (i + 1) * TILE)

    def lanes(v):
        return slice(v * LANES, (v + 1) * LANES)

    work[:LANES, :LANES] = gram_ref[:LANES, :]
    work[:LANES, LANES:] = gram_ref[LANES:2 * LANES, :]
    work[LANES:, :LANES] = jnp.zeros((width - LANES, LANES), f32)
    work[LANES:, LANES:] = gram_ref[2 * LANES:, :]
    row_id = lax.broadcasted_iota(jnp.int32, (width, width), 0)
    col_id = lax.broadcasted_iota(jnp.int32, (width, width), 1)
    identity = (row_id == col_id).astype(f32)
    inverse[...] = identity
    tri_ref[...] = jnp.zeros_like(tri_ref)
    right_ref[0] = identity.astype(BF16)
    right_ref[1] = jnp.zeros((width, width), BF16)
    right_ref[2] = jnp.zeros((width, width), BF16)

    def pass_right():
        left = pieces(inverse[:LOW, :LOW])
        right = pieces(tri_ref[:LOW, :])
        left = jnp.concatenate([left[p] for p, q in TERMS], axis=0)
        right = jnp.concatenate([right[q] for p, q in TERMS], axis=0)
        taken = lax.dot_general(left, right, (((0,), (0,)), ((), ())), preferred_element_type=f32)
        for p, piece in enumerate(pieces(identity[:LOW] - taken)):
            right_ref[p, :LOW, :] = piece

    def finish_pass(c, size):
        here = slice(c * size, (c + 1) * size)
        right = [right_ref[p] for p in range(3)]
        pass_ref[here, :] = product([ref[here, :] for ref in data], right, ((1,), (0,)))

    def finish_basis(c, half, size):
        here = slice(c * size, (c + 1) * size)
        depth = (half + 1) * LANES
        right = [right_ref[p, :LANES, :depth] for p in range(3)]
        basis_ref[here, lanes(half)] = product([ref[here, :depth] for ref in data], right, ((1,), (1,)))

    def basis_right(half):
        depth = (half + 1) * LANES
        for p, piece in enumerate(pieces(inverse[lanes(half), :depth])):
            right_ref[p, :LANES, :depth] = piece

    fillers = []
    pending = None

    for k in range(blocks):
        t = k // per_lanes
        base = (k % per_lanes) * TILE
        s = k // group
        last = min((s + 2) * group, blocks)
        row = {}
        for j in range(TILE):
            r = k * TILE + j
            for v in range(t, width // LANES):
                row["g", v, j] = jnp.broadcast_to(work[r:r + 1, lanes(v)], shape)
            for v in range(0, t + 1):
                row["x", v, j] = jnp.broadcast_to(inverse[r:r + 1, lanes(v)], shape)
        items = [("g", v) for v in range(t, width // LANES)] + [("x", v) for v in range(0, t + 1)]
        a = {}
        for j in range(TILE):
            for m in range(j, TILE):
                a[j, m] = jnp.broadcast_to(row["g", t, j][:, base + m:base + m + 1], shape)
        col = {}
        for i in range(k + 1, last):
            v = i // per_lanes
            if i < (s + 1) * group:
                tile = work[band(i), lanes(v)]
                for j in range(TILE):
                    col[i, j] = jnp.broadcast_to(tile[:, base + j:base + j + 1], shape)
            else:
                here = lane == sub + (i % per_lanes) * TILE
                for j in range(TILE):
                    picked = jnp.where(here, row["g", v, j], 0.0)
                    col[i, j] = jnp.broadcast_to(jnp.sum(picked, axis=1, keepdims=True), shape)
        for j in range(TILE):
            scale = lax.rsqrt(a[j, j])
            for m in range(j + 1, TILE):
                a[j, m] = a[j, m] * scale
            for m in range(j + 1, TILE):
                for p in range(m, TILE):
                    a[m, p] = a[m, p] - a[j, m] * a[j, p]
            for i in range(k + 1, last):
                col[i, j] = col[i, j] * scale
                for m in range(j + 1, TILE):
                    col[i, m] = col[i, m] - a[j, m] * col[i, j]
            for kind, v in items:
                row[kind, v, j] = row[kind, v, j] * scale
                for m in range(j + 1, TILE):
                    row[kind, v, m] = row[kind, v, m] - a[j, m] * row[kind, v, j]
        for i in range(k + 1, last):
            for kind, v in items:
                ref = work if kind == "g" else inverse
                change = [col[i, j] * row[kind, v, j] for j in range(TILE)]
                while len(change) > 1:
                    change = [p + q for p, q in zip(change[::2], change[1::2])]
                ref[band(i), lanes(v)] = ref[band(i), lanes(v)] - change[0]
        for kind, v in items:
            tile = row[kind, v, TILE - 1]
            for j in range(TILE - 2, -1, -1):
                tile = jnp.where(sub == j, row[kind, v, j], tile)
            if kind == "g":
                if v == t:
                    tile = jnp.where(lane >= sub + base, tile, 0.0)
                tri_ref[band(k), lanes(v)] = tile
            else:
                inverse[band(k), lanes(v)] = tile

        if (k + 1) % group == 0:
            if pending is not None:
                at, low, span, drop, fill = pending
                work[at:, low:] = work[at:, low:] - drop
                inverse[at:, :span] = inverse[at:, :span] - fill
                pending = None
            at = (s + 2) * group * TILE
            if at < width:
                done = slice(s * group * TILE, (s + 1) * group * TILE)
                first = (at // LANES) * LANES
                low = first
                span = (t + 1) * LANES
                rest = tri_ref[done, :]
                top = pieces(rest)
                side = pieces(inverse[done, :span])
                left = jnp.concatenate([top[p][:, first:] for p, q in TERMS], axis=0)
                right = jnp.concatenate([top[q][:, low:] for p, q in TERMS], axis=0)
                dims = (((0,), (0,)), ((), ()))
                drop = lax.dot_general(left, right, dims, preferred_element_type=f32)
                right = jnp.concatenate([side[q] for p, q in TERMS], axis=0)
                fill = lax.dot_general(left, right, dims, preferred_element_type=f32)
                pending = at, low, span, drop[at - first:], fill[at - first:]
        if (k + 1) * TILE == LOW:
            fillers.append(pass_right)
            fillers += [functools.partial(finish_pass, c, chunk) for c in range(rows // chunk)]
        if (k + 1) * TILE == LANES:
            fillers.append(functools.partial(basis_right, 0))
            fillers += [functools.partial(finish_basis, c, 0, chunk) for c in range(rows // chunk)]
        if fillers:
            fillers.pop(0)()
    fillers.append(functools.partial(basis_right, 1))
    for c in range(rows // tail):
        fillers.append(functools.partial(finish_basis, c, 1, tail))
    for filler in fillers:
        filler()


def factor_call(gram, high, middle, low, group=2, chunk=128, tail=256):
    rows, width = high.shape
    f32 = jnp.float32
    vmem = pl.BlockSpec(memory_space=pltpu.VMEM)
    square = pltpu.VMEM((width, width), f32)
    return pl.pallas_call(
        functools.partial(factor_kernel, group, chunk, tail),
        out_shape=(
            jax.ShapeDtypeStruct((rows, width), f32),
            jax.ShapeDtypeStruct((width, width), f32),
            jax.ShapeDtypeStruct((rows, width), f32),
        ),
        in_specs=[vmem] * 4,
        out_specs=(vmem, vmem, vmem),
        scratch_shapes=[square, square, pltpu.VMEM((3, width, width), BF16)],
        name="factor",
    )(gram, high, middle, low)


def on_device(sizes, snapshots, live_rows, column_order):
    gram, *masked = masked_and_gram(snapshots, live_rows, column_order, sizes)
    return factor_call(gram, *masked)


def solution(mesh):
    placed = (P(("lon", "lat", "depth"), None), P(("lon", "lat", "depth")), P())
    sizes = (mesh.shape["lon"] // CORES, mesh.shape["lat"], mesh.shape["depth"])
    return jax.shard_map(
        functools.partial(on_device, sizes),
        mesh=mesh,
        in_specs=placed,
        out_specs=(P(("lon", "lat", "depth"), None), P(), P(("lon", "lat", "depth"), None)),
        check_vma=False,
    )
```

```python
import functools

import jax
import jax.numpy as jnp
from jax import lax
from jax.experimental import pallas as pl
from jax.experimental.pallas import tpu as pltpu
from jax.sharding import PartitionSpec as P

LOW = 32
CORES = 2
LANES = 128
TILE = 8
UNIT = 4
LOADS = 4
BF16 = jnp.bfloat16
TERMS = ((2, 0), (0, 2), (1, 1), (1, 0), (0, 1), (0, 0))
HIGHEST = lax.Precision.HIGHEST


def hops(d, n):
    return min(d % n, n - d % n)


def gram_kernel(total_rows, ny, nz, nx, snap_hbm, live_ref, order_ref, out_ref, high_hbm, middle_hbm, low_hbm,
                snap, high_ref, middle_ref, low_ref, gram, from_core, half, from_plane, strip, from_z,
                load_sem, store_sem, line_sem, send_sem, recv_sem):
    rows, width = snap.shape
    lon = lax.axis_index("lon")
    core, y = lax.rem(lon, CORES), lax.div(lon, CORES)
    z, x = lax.axis_index("lat"), lax.axis_index("depth")
    f32 = jnp.float32
    data = (high_ref, middle_ref, low_ref)
    data_hbm = (high_hbm, middle_hbm, low_hbm)

    plane = [(dy, dx) for dy in range(ny) for dx in range(nx) if dy or dx]
    plane.sort(key=lambda d: -hops(d[0], ny) - hops(d[1], nx))
    line = sorted(range(1, nz), key=lambda d: -hops(d, nz))

    def other_core():
        return {"lon": y * CORES + 1 - core}

    def in_plane(dy, dx):
        return lax.rem(y + dy, ny), lax.rem(x + dx, nx)

    def at_plane(dy, dx):
        ty, tx = in_plane(dy, dx)
        return {"lon": ty * CORES + core, "depth": tx}

    def at_z(d):
        return {"lat": lax.rem(z + d, nz)}

    size = rows // LOADS
    loads = []
    for c in range(LOADS):
        here = pl.ds(c * size, size)
        load = pltpu.make_async_copy(snap_hbm.at[here], snap.at[here], load_sem.at[c])
        load.start()
        loads.append(load)

    reach = -(-nz // 4)
    near = [d for d in line if hops(d, nz) <= reach]
    ends = (reach, nz - reach)
    peers = [at_plane(*d) for d in plane] + [at_z(d) for d in near] + [other_core()]
    barrier = pltpu.get_barrier_semaphore()
    for peer in peers:
        pl.semaphore_signal(barrier, inc=1, device_id=peer, device_id_type=pl.DeviceIdType.MESH)

    select = (lax.broadcasted_iota(jnp.int32, (width, width), 0) == order_ref[...]).astype(BF16)
    for c in range(LOADS):
        loads[c].wait()
        here = slice(c * size, (c + 1) * size)
        live = lax.broadcasted_iota(jnp.int32, (size, width), 0) + c * size < live_ref[0]
        for piece, ref in zip(pieces(jnp.where(live, snap[here, :], 0.0)), data):
            ref[here, :] = jnp.dot(piece, select, preferred_element_type=f32).astype(BF16)
    stores = []
    for p, (src, dst) in enumerate(zip(data, data_hbm)):
        store = pltpu.make_async_copy(src, dst, store_sem.at[p])
        store.start()
        stores.append(store)

    def inner(a, b):
        return lax.dot_general(a, b, (((0,), (0,)), ((), ())), preferred_element_type=f32)

    high, middle, low = (ref[...] for ref in data)
    cross = inner(high, low) + inner(high, middle)
    whole = (inner(middle, middle) + (cross + cross.T) + inner(high, high)) * (1.0 / total_rows)

    blocks = (whole[:LANES, :LANES], whole[:LANES, LANES:], whole[LANES:, LANES:])
    per_block = LANES // UNIT
    for at, block in enumerate(blocks):
        gram[at * per_block:(at + 1) * per_block] = block.reshape(per_block, UNIT, LANES)

    pl.semaphore_wait(barrier, len(peers))
    for d in ends:
        pl.semaphore_signal(line_sem, inc=1, device_id=at_z(d), device_id_type=pl.DeviceIdType.MESH)

    used = [0]

    def send(src, dst, peer):
        k = used[0]
        used[0] += 1
        copy = pltpu.make_async_remote_copy(
            src_ref=src, dst_ref=dst, send_sem=send_sem.at[k], recv_sem=recv_sem.at[k],
            device_id=peer, device_id_type=pl.DeviceIdType.MESH,
        )
        copy.start()
        return copy

    places = ny * nx
    n_half = half.shape[0]
    n_strip = n_half // places
    place = y * nx + x

    copy = send(gram.at[pl.ds((1 - core) * n_half, n_half)], from_core, other_core())
    copy.wait()
    half[...] = gram[pl.ds(core * n_half, n_half)] + from_core[...]

    copies = []
    for d in plane:
        ty, tx = in_plane(*d)
        copies.append(send(half.at[pl.ds((ty * nx + tx) * n_strip, n_strip)], from_plane.at[place], at_plane(*d)))
    from_plane[place] = half[pl.ds(place * n_strip, n_strip)]
    for copy in copies:
        copy.wait()
    total = from_plane[0]
    for s in range(1, places):
        total = total + from_plane[s]
    strip[...] = total

    pl.semaphore_wait(line_sem, len(ends))
    copies = [send(strip, from_z.at[z], at_z(d)) for d in line]
    from_z[z] = strip[...]
    for copy in copies:
        copy.wait()
    total = from_z[0]
    for s in range(1, nz):
        total = total + from_z[s]

    def strip_of(p):
        return out_ref.at[pl.ds((core * places + p) * n_strip, n_strip)]

    out_ref[pl.ds((core * places + place) * n_strip, n_strip)] = total
    spread = [send(strip_of(place), strip_of(place), at_plane(*d)) for d in plane]
    handed = [send(strip_of(place), strip_of(place), other_core())]
    for (dy, dx), copy in zip(reversed(plane), reversed(spread)):
        copy.wait_recv()
        source = lax.rem(y + ny - dy, ny) * nx + lax.rem(x + nx - dx, nx)
        handed.append(send(strip_of(source), strip_of(source), other_core()))
    for copy in spread:
        copy.wait_send()
    for copy in handed:
        copy.wait()
    for store in stores:
        store.wait()


def masked_and_gram(snapshots, live_rows, column_order, sizes):
    rows, width = snapshots.shape
    ny, nz, nx = sizes
    places = ny * nx
    units = 3 * LANES // UNIT
    n_half = units // CORES
    n_strip = n_half // places
    copies = 1 + 2 * (places - 1) + (nz - 1) + places
    total_rows = rows * CORES * places * nz
    f32 = jnp.float32
    tile = (UNIT, LANES)
    gram, *masked = pl.pallas_call(
        functools.partial(gram_kernel, total_rows, ny, nz, nx),
        out_shape=(
            jax.ShapeDtypeStruct((units, *tile), f32),
            *[jax.ShapeDtypeStruct((rows, width), BF16)] * 3,
        ),
        in_specs=[
            pl.BlockSpec(memory_space=pl.ANY),
            pl.BlockSpec(memory_space=pltpu.SMEM),
            pl.BlockSpec(memory_space=pltpu.VMEM),
        ],
        out_specs=(pl.BlockSpec(memory_space=pltpu.VMEM), *[pl.BlockSpec(memory_space=pl.ANY)] * 3),
        scratch_shapes=[
            pltpu.VMEM((rows, width), f32),
            *[pltpu.VMEM((rows, width), BF16)] * 3,
            pltpu.VMEM((units, *tile), f32),
            pltpu.VMEM((n_half, *tile), f32),
            pltpu.VMEM((n_half, *tile), f32),
            pltpu.VMEM((places, n_strip, *tile), f32),
            pltpu.VMEM((n_strip, *tile), f32),
            pltpu.VMEM((nz, n_strip, *tile), f32),
            pltpu.SemaphoreType.DMA((LOADS,)),
            pltpu.SemaphoreType.DMA((3,)),
            pltpu.SemaphoreType.REGULAR,
            pltpu.SemaphoreType.DMA((copies,)),
            pltpu.SemaphoreType.DMA((copies,)),
        ],
        compiler_params=pltpu.CompilerParams(collective_id=0, has_side_effects=True),
        name="gram_allreduce",
    )(snapshots, live_rows, column_order.reshape(1, width))
    return gram.reshape(3 * LANES, LANES), *masked


def pieces(value):
    high = value.astype(BF16)
    rest = value - high.astype(jnp.float32)
    middle = rest.astype(BF16)
    return high, middle, (rest - middle.astype(jnp.float32)).astype(BF16)


def product(a, b, dims):
    out = None
    for p, q in TERMS:
        term = lax.dot_general(a[p], b[q], (dims, ((), ())), preferred_element_type=jnp.float32)
        out = term if out is None else out + term
    return out


def factor_kernel(group, chunk, tail, gram_ref, high_ref, middle_ref, low_ref, basis_ref, tri_ref, pass_ref, work, inverse, right_ref):
    rows, width = high_ref.shape
    blocks = width // TILE
    per_lanes = LANES // TILE
    f32 = jnp.float32
    shape = (TILE, LANES)
    sub = lax.broadcasted_iota(jnp.int32, shape, 0)
    lane = lax.broadcasted_iota(jnp.int32, shape, 1)
    data = (high_ref, middle_ref, low_ref)

    def band(i):
        return slice(i * TILE, (i + 1) * TILE)

    def lanes(v):
        return slice(v * LANES, (v + 1) * LANES)

    work[:LANES, :LANES] = gram_ref[:LANES, :]
    work[:LANES, LANES:] = gram_ref[LANES:2 * LANES, :]
    work[LANES:, :LANES] = jnp.zeros((width - LANES, LANES), f32)
    work[LANES:, LANES:] = gram_ref[2 * LANES:, :]
    row_id = lax.broadcasted_iota(jnp.int32, (width, width), 0)
    col_id = lax.broadcasted_iota(jnp.int32, (width, width), 1)
    identity = (row_id == col_id).astype(f32)
    inverse[...] = identity
    tri_ref[...] = jnp.zeros_like(tri_ref)
    right_ref[0] = identity.astype(BF16)
    right_ref[1] = jnp.zeros((width, width), BF16)
    right_ref[2] = jnp.zeros((width, width), BF16)

    def pass_right():
        left = pieces(inverse[:LOW, :LOW])
        right = pieces(tri_ref[:LOW, :])
        left = jnp.concatenate([left[p] for p, q in TERMS], axis=0)
        right = jnp.concatenate([right[q] for p, q in TERMS], axis=0)
        taken = lax.dot_general(left, right, (((0,), (0,)), ((), ())), preferred_element_type=f32)
        for p, piece in enumerate(pieces(identity[:LOW] - taken)):
            right_ref[p, :LOW, :] = piece

    def finish_pass(c, size):
        here = slice(c * size, (c + 1) * size)
        right = [right_ref[p] for p in range(3)]
        pass_ref[here, :] = product([ref[here, :] for ref in data], right, ((1,), (0,)))

    def finish_basis(c, half, size):
        here = slice(c * size, (c + 1) * size)
        depth = (half + 1) * LANES
        right = [right_ref[p, :LANES, :depth] for p in range(3)]
        basis_ref[here, lanes(half)] = product([ref[here, :depth] for ref in data], right, ((1,), (1,)))

    def basis_right(half):
        depth = (half + 1) * LANES
        for p, piece in enumerate(pieces(inverse[lanes(half), :depth])):
            right_ref[p, :LANES, :depth] = piece

    fillers = []
    pending = None

    for k in range(blocks):
        t = k // per_lanes
        base = (k % per_lanes) * TILE
        s = k // group
        last = min((s + 2) * group, blocks)
        row = {}
        for j in range(TILE):
            r = k * TILE + j
            for v in range(t, width // LANES):
                row["g", v, j] = jnp.broadcast_to(work[r:r + 1, lanes(v)], shape)
            for v in range(0, t + 1):
                row["x", v, j] = jnp.broadcast_to(inverse[r:r + 1, lanes(v)], shape)
        items = [("g", v) for v in range(t, width // LANES)] + [("x", v) for v in range(0, t + 1)]
        a = {}
        for j in range(TILE):
            for m in range(j, TILE):
                a[j, m] = jnp.broadcast_to(row["g", t, j][:, base + m:base + m + 1], shape)
        col = {}
        for i in range(k + 1, last):
            v = i // per_lanes
            if i < (s + 1) * group:
                tile = work[band(i), lanes(v)]
                for j in range(TILE):
                    col[i, j] = jnp.broadcast_to(tile[:, base + j:base + j + 1], shape)
            else:
                here = lane == sub + (i % per_lanes) * TILE
                for j in range(TILE):
                    picked = jnp.where(here, row["g", v, j], 0.0)
                    col[i, j] = jnp.broadcast_to(jnp.sum(picked, axis=1, keepdims=True), shape)
        for j in range(TILE):
            scale = lax.rsqrt(a[j, j])
            for m in range(j + 1, TILE):
                a[j, m] = a[j, m] * scale
            for m in range(j + 1, TILE):
                for p in range(m, TILE):
                    a[m, p] = a[m, p] - a[j, m] * a[j, p]
            for i in range(k + 1, last):
                col[i, j] = col[i, j] * scale
                for m in range(j + 1, TILE):
                    col[i, m] = col[i, m] - a[j, m] * col[i, j]
            for kind, v in items:
                row[kind, v, j] = row[kind, v, j] * scale
                for m in range(j + 1, TILE):
                    row[kind, v, m] = row[kind, v, m] - a[j, m] * row[kind, v, j]
        for i in range(k + 1, last):
            for kind, v in items:
                ref = work if kind == "g" else inverse
                change = [col[i, j] * row[kind, v, j] for j in range(TILE)]
                while len(change) > 1:
                    change = [p + q for p, q in zip(change[::2], change[1::2])]
                ref[band(i), lanes(v)] = ref[band(i), lanes(v)] - change[0]
        for kind, v in items:
            tile = row[kind, v, TILE - 1]
            for j in range(TILE - 2, -1, -1):
                tile = jnp.where(sub == j, row[kind, v, j], tile)
            if kind == "g":
                if v == t:
                    tile = jnp.where(lane >= sub + base, tile, 0.0)
                tri_ref[band(k), lanes(v)] = tile
            else:
                inverse[band(k), lanes(v)] = tile

        if (k + 1) % group == 0:
            if pending is not None:
                at, low, span, drop, fill = pending
                work[at:, low:] = work[at:, low:] - drop
                inverse[at:, :span] = inverse[at:, :span] - fill
                pending = None
            at = (s + 2) * group * TILE
            if at < width:
                done = slice(s * group * TILE, (s + 1) * group * TILE)
                first = (at // LANES) * LANES
                low = first
                span = (t + 1) * LANES
                rest = tri_ref[done, :]
                top = pieces(rest)
                side = pieces(inverse[done, :span])
                left = jnp.concatenate([top[p][:, first:] for p, q in TERMS], axis=0)
                right = jnp.concatenate([top[q][:, low:] for p, q in TERMS], axis=0)
                dims = (((0,), (0,)), ((), ()))
                drop = lax.dot_general(left, right, dims, preferred_element_type=f32)
                right = jnp.concatenate([side[q] for p, q in TERMS], axis=0)
                fill = lax.dot_general(left, right, dims, preferred_element_type=f32)
                pending = at, low, span, drop[at - first:], fill[at - first:]
        if (k + 1) * TILE == LOW:
            fillers.append(pass_right)
            fillers += [functools.partial(finish_pass, c, chunk) for c in range(rows // chunk)]
        if (k + 1) * TILE == LANES:
            fillers.append(functools.partial(basis_right, 0))
            fillers += [functools.partial(finish_basis, c, 0, chunk) for c in range(rows // chunk)]
        if fillers:
            fillers.pop(0)()
    fillers.append(functools.partial(basis_right, 1))
    for c in range(rows // tail):
        fillers.append(functools.partial(finish_basis, c, 1, tail))
    for filler in fillers:
        filler()


def factor_call(gram, high, middle, low, group=2, chunk=128, tail=256):
    rows, width = high.shape
    f32 = jnp.float32
    vmem = pl.BlockSpec(memory_space=pltpu.VMEM)
    square = pltpu.VMEM((width, width), f32)
    return pl.pallas_call(
        functools.partial(factor_kernel, group, chunk, tail),
        out_shape=(
            jax.ShapeDtypeStruct((rows, width), f32),
            jax.ShapeDtypeStruct((width, width), f32),
            jax.ShapeDtypeStruct((rows, width), f32),
        ),
        in_specs=[vmem] * 4,
        out_specs=(vmem, vmem, vmem),
        scratch_shapes=[square, square, pltpu.VMEM((3, width, width), BF16)],
        name="factor",
    )(gram, high, middle, low)


def on_device(sizes, snapshots, live_rows, column_order):
    gram, *masked = masked_and_gram(snapshots, live_rows, column_order, sizes)
    return factor_call(gram, *masked)


def solution(mesh):
    placed = (P(("lon", "lat", "depth"), None), P(("lon", "lat", "depth")), P())
    sizes = (mesh.shape["lon"] // CORES, mesh.shape["lat"], mesh.shape["depth"])
    return jax.shard_map(
        functools.partial(on_device, sizes),
        mesh=mesh,
        in_specs=placed,
        out_specs=(P(("lon", "lat", "depth"), None), P(), P(("lon", "lat", "depth"), None)),
        check_vma=False,
    )
```

```python
import functools

import jax
import jax.numpy as jnp
from jax import lax
from jax.experimental import pallas as pl
from jax.experimental.pallas import tpu as pltpu
from jax.sharding import PartitionSpec as P

LOW = 32
CORES = 2
LANES = 128
TILE = 8
UNIT = 4
LOADS = 4
VMEM_LIMIT = 24 * 2**20
BF16 = jnp.bfloat16
TERMS = ((2, 0), (0, 2), (1, 1), (1, 0), (0, 1), (0, 0))
HIGHEST = lax.Precision.HIGHEST


def hops(d, n):
    return min(d % n, n - d % n)


def gram_kernel(total_rows, ny, nz, nx, snap_hbm, live_ref, order_hbm, out_ref, high_ref, middle_ref, low_ref,
                snap, order_ref, gram, from_core, half, from_plane, strip, from_z,
                load_sem, small_sem, line_sem, send_sem, recv_sem):
    rows, width = snap.shape
    lon = lax.axis_index("lon")
    core, y = lax.rem(lon, CORES), lax.div(lon, CORES)
    z, x = lax.axis_index("lat"), lax.axis_index("depth")
    f32 = jnp.float32
    data = (high_ref, middle_ref, low_ref)

    plane = [(dy, dx) for dy in range(ny) for dx in range(nx) if dy or dx]
    plane.sort(key=lambda d: -hops(d[0], ny) - hops(d[1], nx))
    line = sorted(range(1, nz), key=lambda d: -hops(d, nz))

    def other_core():
        return {"lon": y * CORES + 1 - core}

    def in_plane(dy, dx):
        return lax.rem(y + dy, ny), lax.rem(x + dx, nx)

    def at_plane(dy, dx):
        ty, tx = in_plane(dy, dx)
        return {"lon": ty * CORES + core, "depth": tx}

    def at_z(d):
        return {"lat": lax.rem(z + d, nz)}

    picks = pltpu.make_async_copy(order_hbm, order_ref, small_sem)
    picks.start()
    size = rows // LOADS
    loads = []
    for c in range(LOADS):
        here = pl.ds(c * size, size)
        load = pltpu.make_async_copy(snap_hbm.at[here], snap.at[here], load_sem.at[c])
        load.start()
        loads.append(load)

    reach = -(-nz // 4)
    near = [d for d in line if hops(d, nz) <= reach]
    ends = (reach, nz - reach)
    peers = [at_plane(*d) for d in plane] + [at_z(d) for d in near] + [other_core()]
    barrier = pltpu.get_barrier_semaphore()
    for peer in peers:
        pl.semaphore_signal(barrier, inc=1, device_id=peer, device_id_type=pl.DeviceIdType.MESH)

    picks.wait()
    select = (lax.broadcasted_iota(jnp.int32, (width, width), 0) == order_ref[...]).astype(BF16)
    for c in range(LOADS):
        loads[c].wait()
        here = slice(c * size, (c + 1) * size)
        live = lax.broadcasted_iota(jnp.int32, (size, width), 0) + c * size < live_ref[0]
        for piece, ref in zip(pieces(jnp.where(live, snap[here, :], 0.0)), data):
            ref[here, :] = jnp.dot(piece, select, preferred_element_type=f32).astype(BF16)
    def inner(a, b):
        return lax.dot_general(a, b, (((0,), (0,)), ((), ())), preferred_element_type=f32)

    high, middle, low = (ref[...] for ref in data)
    cross = inner(high, low) + inner(high, middle)
    whole = (inner(middle, middle) + (cross + cross.T) + inner(high, high)) * (1.0 / total_rows)

    blocks = (whole[:LANES, :LANES], whole[:LANES, LANES:], whole[LANES:, LANES:])
    per_block = LANES // UNIT
    for at, block in enumerate(blocks):
        gram[at * per_block:(at + 1) * per_block] = block.reshape(per_block, UNIT, LANES)

    pl.semaphore_wait(barrier, len(peers))
    for d in ends:
        pl.semaphore_signal(line_sem, inc=1, device_id=at_z(d), device_id_type=pl.DeviceIdType.MESH)

    used = [0]

    def send(src, dst, peer):
        k = used[0]
        used[0] += 1
        copy = pltpu.make_async_remote_copy(
            src_ref=src, dst_ref=dst, send_sem=send_sem.at[k], recv_sem=recv_sem.at[k],
            device_id=peer, device_id_type=pl.DeviceIdType.MESH,
        )
        copy.start()
        return copy

    places = ny * nx
    n_half = half.shape[0]
    n_strip = n_half // places
    place = y * nx + x

    copy = send(gram.at[pl.ds((1 - core) * n_half, n_half)], from_core, other_core())
    copy.wait()
    half[...] = gram[pl.ds(core * n_half, n_half)] + from_core[...]

    copies = []
    for d in plane:
        ty, tx = in_plane(*d)
        copies.append(send(half.at[pl.ds((ty * nx + tx) * n_strip, n_strip)], from_plane.at[place], at_plane(*d)))
    from_plane[place] = half[pl.ds(place * n_strip, n_strip)]
    for copy in copies:
        copy.wait()
    total = from_plane[0]
    for s in range(1, places):
        total = total + from_plane[s]
    strip[...] = total

    pl.semaphore_wait(line_sem, len(ends))
    copies = [send(strip, from_z.at[z], at_z(d)) for d in line]
    from_z[z] = strip[...]
    for copy in copies:
        copy.wait()
    total = from_z[0]
    for s in range(1, nz):
        total = total + from_z[s]

    def strip_of(p):
        return out_ref.at[pl.ds((core * places + p) * n_strip, n_strip)]

    out_ref[pl.ds((core * places + place) * n_strip, n_strip)] = total
    spread = [send(strip_of(place), strip_of(place), at_plane(*d)) for d in plane]
    handed = [send(strip_of(place), strip_of(place), other_core())]
    for (dy, dx), copy in zip(reversed(plane), reversed(spread)):
        copy.wait_recv()
        source = lax.rem(y + ny - dy, ny) * nx + lax.rem(x + nx - dx, nx)
        handed.append(send(strip_of(source), strip_of(source), other_core()))
    for copy in spread:
        copy.wait_send()
    for copy in handed:
        copy.wait()


def masked_and_gram(snapshots, live_rows, column_order, sizes):
    rows, width = snapshots.shape
    ny, nz, nx = sizes
    places = ny * nx
    units = 3 * LANES // UNIT
    n_half = units // CORES
    n_strip = n_half // places
    copies = 1 + 2 * (places - 1) + (nz - 1) + places
    total_rows = rows * CORES * places * nz
    f32 = jnp.float32
    tile = (UNIT, LANES)

    def in_hbm(array):
        return pltpu.with_memory_space_constraint(array, pltpu.HBM)

    gram, *masked = pl.pallas_call(
        functools.partial(gram_kernel, total_rows, ny, nz, nx),
        out_shape=(
            jax.ShapeDtypeStruct((units, *tile), f32),
            *[jax.ShapeDtypeStruct((rows, width), BF16)] * 3,
        ),
        in_specs=[
            pl.BlockSpec(memory_space=pltpu.HBM),
            pl.BlockSpec(memory_space=pltpu.SMEM),
            pl.BlockSpec(memory_space=pltpu.HBM),
        ],
        out_specs=(pl.BlockSpec(memory_space=pltpu.VMEM),) * 4,
        scratch_shapes=[
            pltpu.VMEM((rows, width), f32),
            pltpu.VMEM((1, width), jnp.int32),
            pltpu.VMEM((units, *tile), f32),
            pltpu.VMEM((n_half, *tile), f32),
            pltpu.VMEM((n_half, *tile), f32),
            pltpu.VMEM((places, n_strip, *tile), f32),
            pltpu.VMEM((n_strip, *tile), f32),
            pltpu.VMEM((nz, n_strip, *tile), f32),
            pltpu.SemaphoreType.DMA((LOADS,)),
            pltpu.SemaphoreType.DMA,
            pltpu.SemaphoreType.REGULAR,
            pltpu.SemaphoreType.DMA((copies,)),
            pltpu.SemaphoreType.DMA((copies,)),
        ],
        compiler_params=pltpu.CompilerParams(collective_id=0, has_side_effects=True, vmem_limit_bytes=VMEM_LIMIT),
        name="gram_allreduce",
    )(in_hbm(snapshots), live_rows, in_hbm(column_order.reshape(1, width)))
    return gram.reshape(3 * LANES, LANES), *masked


def pieces(value):
    high = value.astype(BF16)
    rest = value - high.astype(jnp.float32)
    middle = rest.astype(BF16)
    return high, middle, (rest - middle.astype(jnp.float32)).astype(BF16)


def product(a, b, dims):
    out = None
    for p, q in TERMS:
        term = lax.dot_general(a[p], b[q], (dims, ((), ())), preferred_element_type=jnp.float32)
        out = term if out is None else out + term
    return out


def factor_kernel(group, chunk, tail, gram_ref, high_ref, middle_ref, low_ref, basis_ref, tri_ref, pass_ref, work, inverse, right_ref):
    rows, width = high_ref.shape
    blocks = width // TILE
    per_lanes = LANES // TILE
    f32 = jnp.float32
    shape = (TILE, LANES)
    sub = lax.broadcasted_iota(jnp.int32, shape, 0)
    lane = lax.broadcasted_iota(jnp.int32, shape, 1)
    data = (high_ref, middle_ref, low_ref)

    def band(i):
        return slice(i * TILE, (i + 1) * TILE)

    def lanes(v):
        return slice(v * LANES, (v + 1) * LANES)

    work[:LANES, :LANES] = gram_ref[:LANES, :]
    work[:LANES, LANES:] = gram_ref[LANES:2 * LANES, :]
    work[LANES:, :LANES] = jnp.zeros((width - LANES, LANES), f32)
    work[LANES:, LANES:] = gram_ref[2 * LANES:, :]
    row_id = lax.broadcasted_iota(jnp.int32, (width, width), 0)
    col_id = lax.broadcasted_iota(jnp.int32, (width, width), 1)
    identity = (row_id == col_id).astype(f32)
    inverse[...] = identity
    tri_ref[...] = jnp.zeros_like(tri_ref)
    right_ref[0] = identity.astype(BF16)
    right_ref[1] = jnp.zeros((width, width), BF16)
    right_ref[2] = jnp.zeros((width, width), BF16)

    def pass_right():
        left = pieces(inverse[:LOW, :LOW])
        right = pieces(tri_ref[:LOW, :])
        left = jnp.concatenate([left[p] for p, q in TERMS], axis=0)
        right = jnp.concatenate([right[q] for p, q in TERMS], axis=0)
        taken = lax.dot_general(left, right, (((0,), (0,)), ((), ())), preferred_element_type=f32)
        for p, piece in enumerate(pieces(identity[:LOW] - taken)):
            right_ref[p, :LOW, :] = piece

    def finish_pass(c, size):
        here = slice(c * size, (c + 1) * size)
        right = [right_ref[p] for p in range(3)]
        pass_ref[here, :] = product([ref[here, :] for ref in data], right, ((1,), (0,)))

    def finish_basis(c, half, size):
        here = slice(c * size, (c + 1) * size)
        depth = (half + 1) * LANES
        right = [right_ref[p, :LANES, :depth] for p in range(3)]
        basis_ref[here, lanes(half)] = product([ref[here, :depth] for ref in data], right, ((1,), (1,)))

    def basis_right(half):
        depth = (half + 1) * LANES
        for p, piece in enumerate(pieces(inverse[lanes(half), :depth])):
            right_ref[p, :LANES, :depth] = piece

    fillers = []
    pending = None

    for k in range(blocks):
        t = k // per_lanes
        base = (k % per_lanes) * TILE
        s = k // group
        last = min((s + 2) * group, blocks)
        row = {}
        for j in range(TILE):
            r = k * TILE + j
            for v in range(t, width // LANES):
                row["g", v, j] = jnp.broadcast_to(work[r:r + 1, lanes(v)], shape)
            for v in range(0, t + 1):
                row["x", v, j] = jnp.broadcast_to(inverse[r:r + 1, lanes(v)], shape)
        items = [("g", v) for v in range(t, width // LANES)] + [("x", v) for v in range(0, t + 1)]
        a = {}
        for j in range(TILE):
            for m in range(j, TILE):
                a[j, m] = jnp.broadcast_to(row["g", t, j][:, base + m:base + m + 1], shape)
        col = {}
        for i in range(k + 1, last):
            v = i // per_lanes
            if i < (s + 1) * group:
                tile = work[band(i), lanes(v)]
                for j in range(TILE):
                    col[i, j] = jnp.broadcast_to(tile[:, base + j:base + j + 1], shape)
            else:
                here = lane == sub + (i % per_lanes) * TILE
                for j in range(TILE):
                    picked = jnp.where(here, row["g", v, j], 0.0)
                    col[i, j] = jnp.broadcast_to(jnp.sum(picked, axis=1, keepdims=True), shape)
        for j in range(TILE):
            scale = lax.rsqrt(a[j, j])
            for m in range(j + 1, TILE):
                a[j, m] = a[j, m] * scale
            for m in range(j + 1, TILE):
                for p in range(m, TILE):
                    a[m, p] = a[m, p] - a[j, m] * a[j, p]
            for i in range(k + 1, last):
                col[i, j] = col[i, j] * scale
                for m in range(j + 1, TILE):
                    col[i, m] = col[i, m] - a[j, m] * col[i, j]
            for kind, v in items:
                row[kind, v, j] = row[kind, v, j] * scale
                for m in range(j + 1, TILE):
                    row[kind, v, m] = row[kind, v, m] - a[j, m] * row[kind, v, j]
        for i in range(k + 1, last):
            for kind, v in items:
                ref = work if kind == "g" else inverse
                change = [col[i, j] * row[kind, v, j] for j in range(TILE)]
                while len(change) > 1:
                    change = [p + q for p, q in zip(change[::2], change[1::2])]
                ref[band(i), lanes(v)] = ref[band(i), lanes(v)] - change[0]
        for kind, v in items:
            tile = row[kind, v, TILE - 1]
            for j in range(TILE - 2, -1, -1):
                tile = jnp.where(sub == j, row[kind, v, j], tile)
            if kind == "g":
                if v == t:
                    tile = jnp.where(lane >= sub + base, tile, 0.0)
                tri_ref[band(k), lanes(v)] = tile
            else:
                inverse[band(k), lanes(v)] = tile

        if (k + 1) % group == 0:
            if pending is not None:
                at, low, span, drop, fill = pending
                work[at:, low:] = work[at:, low:] - drop
                inverse[at:, :span] = inverse[at:, :span] - fill
                pending = None
            at = (s + 2) * group * TILE
            if at < width:
                done = slice(s * group * TILE, (s + 1) * group * TILE)
                first = (at // LANES) * LANES
                low = first
                span = (t + 1) * LANES
                rest = tri_ref[done, :]
                top = pieces(rest)
                side = pieces(inverse[done, :span])
                left = jnp.concatenate([top[p][:, first:] for p, q in TERMS], axis=0)
                right = jnp.concatenate([top[q][:, low:] for p, q in TERMS], axis=0)
                dims = (((0,), (0,)), ((), ()))
                drop = lax.dot_general(left, right, dims, preferred_element_type=f32)
                right = jnp.concatenate([side[q] for p, q in TERMS], axis=0)
                fill = lax.dot_general(left, right, dims, preferred_element_type=f32)
                pending = at, low, span, drop[at - first:], fill[at - first:]
        if (k + 1) * TILE == LOW:
            fillers.append(pass_right)
            fillers += [functools.partial(finish_pass, c, chunk) for c in range(rows // chunk)]
        if (k + 1) * TILE == LANES:
            fillers.append(functools.partial(basis_right, 0))
            fillers += [functools.partial(finish_basis, c, 0, chunk) for c in range(rows // chunk)]
        if fillers:
            fillers.pop(0)()
    fillers.append(functools.partial(basis_right, 1))
    for c in range(rows // tail):
        fillers.append(functools.partial(finish_basis, c, 1, tail))
    for filler in fillers:
        filler()


def factor_call(gram, high, middle, low, group=2, chunk=128, tail=256):
    rows, width = high.shape
    f32 = jnp.float32
    vmem = pl.BlockSpec(memory_space=pltpu.VMEM)
    square = pltpu.VMEM((width, width), f32)
    return pl.pallas_call(
        functools.partial(factor_kernel, group, chunk, tail),
        out_shape=(
            jax.ShapeDtypeStruct((rows, width), f32),
            jax.ShapeDtypeStruct((width, width), f32),
            jax.ShapeDtypeStruct((rows, width), f32),
        ),
        in_specs=[vmem] * 4,
        out_specs=(vmem, vmem, vmem),
        scratch_shapes=[square, square, pltpu.VMEM((3, width, width), BF16)],
        compiler_params=pltpu.CompilerParams(vmem_limit_bytes=VMEM_LIMIT),
        name="factor",
    )(gram, high, middle, low)


def on_device(sizes, snapshots, live_rows, column_order):
    gram, *masked = masked_and_gram(snapshots, live_rows, column_order, sizes)
    return factor_call(gram, *masked)


def solution(mesh):
    placed = (P(("lon", "lat", "depth"), None), P(("lon", "lat", "depth")), P())
    sizes = (mesh.shape["lon"] // CORES, mesh.shape["lat"], mesh.shape["depth"])
    return jax.shard_map(
        functools.partial(on_device, sizes),
        mesh=mesh,
        in_specs=placed,
        out_specs=(P(("lon", "lat", "depth"), None), P(), P(("lon", "lat", "depth"), None)),
        check_vma=False,
    )
```

```python
import functools

import jax
import jax.numpy as jnp
from jax import lax
from jax.experimental import pallas as pl
from jax.experimental.pallas import tpu as pltpu
from jax.sharding import PartitionSpec as P

LOW = 32
CORES = 2
LANES = 128
TILE = 8
UNIT = 4
LOADS = 4
VMEM_LIMIT = 24 * 2**20
BF16 = jnp.bfloat16
TERMS = ((2, 0), (0, 2), (1, 1), (1, 0), (0, 1), (0, 0))
HIGHEST = lax.Precision.HIGHEST


def hops(d, n):
    return min(d % n, n - d % n)


def gram_kernel(total_rows, ny, nz, nx, snap_hbm, live_ref, order_hbm, out_ref, high_ref, middle_ref, low_ref,
                snap, order_ref, gram, from_core, half, from_plane, strip, from_z,
                load_sem, small_sem, line_sem, send_sem, recv_sem):
    rows, width = snap.shape
    lon = lax.axis_index("lon")
    core, y = lax.rem(lon, CORES), lax.div(lon, CORES)
    z, x = lax.axis_index("lat"), lax.axis_index("depth")
    f32 = jnp.float32
    data = (high_ref, middle_ref, low_ref)

    plane = [(dy, dx) for dy in range(ny) for dx in range(nx) if dy or dx]
    plane.sort(key=lambda d: -hops(d[0], ny) - hops(d[1], nx))
    line = sorted(range(1, nz), key=lambda d: -hops(d, nz))

    def other_core():
        return {"lon": y * CORES + 1 - core}

    def in_plane(dy, dx):
        return lax.rem(y + dy, ny), lax.rem(x + dx, nx)

    def at_plane(dy, dx):
        ty, tx = in_plane(dy, dx)
        return {"lon": ty * CORES + core, "depth": tx}

    def across(dy, dx):
        ty, tx = in_plane(dy, dx)
        return {"lon": ty * CORES + 1 - core, "depth": tx}

    def at_z(d):
        return {"lat": lax.rem(z + d, nz)}

    picks = pltpu.make_async_copy(order_hbm, order_ref, small_sem)
    picks.start()
    size = rows // LOADS
    loads = []
    for c in range(LOADS):
        here = pl.ds(c * size, size)
        load = pltpu.make_async_copy(snap_hbm.at[here], snap.at[here], load_sem.at[c])
        load.start()
        loads.append(load)

    reach = -(-nz // 4)
    near = [d for d in line if hops(d, nz) <= reach]
    ends = (reach, nz - reach)
    peers = [at_plane(*d) for d in plane] + [across(*d) for d in plane] + [at_z(d) for d in near] + [other_core()]
    barrier = pltpu.get_barrier_semaphore()
    for peer in peers:
        pl.semaphore_signal(barrier, inc=1, device_id=peer, device_id_type=pl.DeviceIdType.MESH)

    picks.wait()
    select = (lax.broadcasted_iota(jnp.int32, (width, width), 0) == order_ref[...]).astype(BF16)
    for c in range(LOADS):
        loads[c].wait()
        here = slice(c * size, (c + 1) * size)
        live = lax.broadcasted_iota(jnp.int32, (size, width), 0) + c * size < live_ref[0]
        for piece, ref in zip(pieces(jnp.where(live, snap[here, :], 0.0)), data):
            ref[here, :] = jnp.dot(piece, select, preferred_element_type=f32).astype(BF16)
    def inner(a, b):
        return lax.dot_general(a, b, (((0,), (0,)), ((), ())), preferred_element_type=f32)

    high, middle, low = (ref[...] for ref in data)
    cross = inner(high, low) + inner(high, middle)
    whole = (inner(middle, middle) + (cross + cross.T) + inner(high, high)) * (1.0 / total_rows)

    blocks = (whole[:LANES, :LANES], whole[:LANES, LANES:], whole[LANES:, LANES:])
    per_block = LANES // UNIT
    for at, block in enumerate(blocks):
        gram[at * per_block:(at + 1) * per_block] = block.reshape(per_block, UNIT, LANES)

    pl.semaphore_wait(barrier, len(peers))
    for d in ends:
        pl.semaphore_signal(line_sem, inc=1, device_id=at_z(d), device_id_type=pl.DeviceIdType.MESH)

    used = [0]

    def send(src, dst, peer):
        k = used[0]
        used[0] += 1
        copy = pltpu.make_async_remote_copy(
            src_ref=src, dst_ref=dst, send_sem=send_sem.at[k], recv_sem=recv_sem.at[k],
            device_id=peer, device_id_type=pl.DeviceIdType.MESH,
        )
        copy.start()
        return copy

    places = ny * nx
    n_half = half.shape[0]
    n_strip = n_half // places
    place = y * nx + x

    copy = send(gram.at[pl.ds((1 - core) * n_half, n_half)], from_core, other_core())
    copy.wait()
    half[...] = gram[pl.ds(core * n_half, n_half)] + from_core[...]

    copies = []
    for d in plane:
        ty, tx = in_plane(*d)
        copies.append(send(half.at[pl.ds((ty * nx + tx) * n_strip, n_strip)], from_plane.at[place], at_plane(*d)))
    from_plane[place] = half[pl.ds(place * n_strip, n_strip)]
    for copy in copies:
        copy.wait()
    total = from_plane[0]
    for s in range(1, places):
        total = total + from_plane[s]
    strip[...] = total

    pl.semaphore_wait(line_sem, len(ends))
    copies = [send(strip, from_z.at[z], at_z(d)) for d in line]
    from_z[z] = strip[...]
    for copy in copies:
        copy.wait()
    total = from_z[0]
    for s in range(1, nz):
        total = total + from_z[s]

    def strip_of(p):
        return out_ref.at[pl.ds((core * places + p) * n_strip, n_strip)]

    out_ref[pl.ds((core * places + place) * n_strip, n_strip)] = total
    copies = []
    for d in plane:
        copies.append(send(strip_of(place), strip_of(place), at_plane(*d)))
        copies.append(send(strip_of(place), strip_of(place), across(*d)))
    copies.append(send(strip_of(place), strip_of(place), other_core()))
    for copy in copies:
        copy.wait()


def masked_and_gram(snapshots, live_rows, column_order, sizes):
    rows, width = snapshots.shape
    ny, nz, nx = sizes
    places = ny * nx
    units = 3 * LANES // UNIT
    n_half = units // CORES
    n_strip = n_half // places
    copies = 2 + 3 * (places - 1) + (nz - 1)
    total_rows = rows * CORES * places * nz
    f32 = jnp.float32
    tile = (UNIT, LANES)

    def in_hbm(array):
        return pltpu.with_memory_space_constraint(array, pltpu.HBM)

    gram, *masked = pl.pallas_call(
        functools.partial(gram_kernel, total_rows, ny, nz, nx),
        out_shape=(
            jax.ShapeDtypeStruct((units, *tile), f32),
            *[jax.ShapeDtypeStruct((rows, width), BF16)] * 3,
        ),
        in_specs=[
            pl.BlockSpec(memory_space=pltpu.HBM),
            pl.BlockSpec(memory_space=pltpu.SMEM),
            pl.BlockSpec(memory_space=pltpu.HBM),
        ],
        out_specs=(pl.BlockSpec(memory_space=pltpu.VMEM),) * 4,
        scratch_shapes=[
            pltpu.VMEM((rows, width), f32),
            pltpu.VMEM((1, width), jnp.int32),
            pltpu.VMEM((units, *tile), f32),
            pltpu.VMEM((n_half, *tile), f32),
            pltpu.VMEM((n_half, *tile), f32),
            pltpu.VMEM((places, n_strip, *tile), f32),
            pltpu.VMEM((n_strip, *tile), f32),
            pltpu.VMEM((nz, n_strip, *tile), f32),
            pltpu.SemaphoreType.DMA((LOADS,)),
            pltpu.SemaphoreType.DMA,
            pltpu.SemaphoreType.REGULAR,
            pltpu.SemaphoreType.DMA((copies,)),
            pltpu.SemaphoreType.DMA((copies,)),
        ],
        compiler_params=pltpu.CompilerParams(collective_id=0, has_side_effects=True, vmem_limit_bytes=VMEM_LIMIT),
        name="gram_allreduce",
    )(in_hbm(snapshots), live_rows, in_hbm(column_order.reshape(1, width)))
    return gram.reshape(3 * LANES, LANES), *masked


def pieces(value):
    high = value.astype(BF16)
    rest = value - high.astype(jnp.float32)
    middle = rest.astype(BF16)
    return high, middle, (rest - middle.astype(jnp.float32)).astype(BF16)


def product(a, b, dims):
    out = None
    for p, q in TERMS:
        term = lax.dot_general(a[p], b[q], (dims, ((), ())), preferred_element_type=jnp.float32)
        out = term if out is None else out + term
    return out


def factor_kernel(group, chunk, tail, gram_ref, high_ref, middle_ref, low_ref, basis_ref, tri_ref, pass_ref, work, inverse, right_ref):
    rows, width = high_ref.shape
    blocks = width // TILE
    per_lanes = LANES // TILE
    f32 = jnp.float32
    shape = (TILE, LANES)
    sub = lax.broadcasted_iota(jnp.int32, shape, 0)
    lane = lax.broadcasted_iota(jnp.int32, shape, 1)
    data = (high_ref, middle_ref, low_ref)

    def band(i):
        return slice(i * TILE, (i + 1) * TILE)

    def lanes(v):
        return slice(v * LANES, (v + 1) * LANES)

    work[:LANES, :LANES] = gram_ref[:LANES, :]
    work[:LANES, LANES:] = gram_ref[LANES:2 * LANES, :]
    work[LANES:, :LANES] = jnp.zeros((width - LANES, LANES), f32)
    work[LANES:, LANES:] = gram_ref[2 * LANES:, :]
    row_id = lax.broadcasted_iota(jnp.int32, (width, width), 0)
    col_id = lax.broadcasted_iota(jnp.int32, (width, width), 1)
    identity = (row_id == col_id).astype(f32)
    inverse[...] = identity
    tri_ref[...] = jnp.zeros_like(tri_ref)
    right_ref[0] = identity.astype(BF16)
    right_ref[1] = jnp.zeros((width, width), BF16)
    right_ref[2] = jnp.zeros((width, width), BF16)

    def pass_right():
        left = pieces(inverse[:LOW, :LOW])
        right = pieces(tri_ref[:LOW, :])
        left = jnp.concatenate([left[p] for p, q in TERMS], axis=0)
        right = jnp.concatenate([right[q] for p, q in TERMS], axis=0)
        taken = lax.dot_general(left, right, (((0,), (0,)), ((), ())), preferred_element_type=f32)
        for p, piece in enumerate(pieces(identity[:LOW] - taken)):
            right_ref[p, :LOW, :] = piece

    def finish_pass(c, size):
        here = slice(c * size, (c + 1) * size)
        right = [right_ref[p] for p in range(3)]
        pass_ref[here, :] = product([ref[here, :] for ref in data], right, ((1,), (0,)))

    def finish_basis(c, half, size):
        here = slice(c * size, (c + 1) * size)
        depth = (half + 1) * LANES
        right = [right_ref[p, :LANES, :depth] for p in range(3)]
        basis_ref[here, lanes(half)] = product([ref[here, :depth] for ref in data], right, ((1,), (1,)))

    def basis_right(half):
        depth = (half + 1) * LANES
        for p, piece in enumerate(pieces(inverse[lanes(half), :depth])):
            right_ref[p, :LANES, :depth] = piece

    fillers = []
    pending = None

    for k in range(blocks):
        t = k // per_lanes
        base = (k % per_lanes) * TILE
        s = k // group
        last = min((s + 2) * group, blocks)
        row = {}
        for j in range(TILE):
            r = k * TILE + j
            for v in range(t, width // LANES):
                row["g", v, j] = jnp.broadcast_to(work[r:r + 1, lanes(v)], shape)
            for v in range(0, t + 1):
                row["x", v, j] = jnp.broadcast_to(inverse[r:r + 1, lanes(v)], shape)
        items = [("g", v) for v in range(t, width // LANES)] + [("x", v) for v in range(0, t + 1)]
        a = {}
        for j in range(TILE):
            for m in range(j, TILE):
                a[j, m] = jnp.broadcast_to(row["g", t, j][:, base + m:base + m + 1], shape)
        col = {}
        for i in range(k + 1, last):
            v = i // per_lanes
            if i < (s + 1) * group:
                tile = work[band(i), lanes(v)]
                for j in range(TILE):
                    col[i, j] = jnp.broadcast_to(tile[:, base + j:base + j + 1], shape)
            else:
                here = lane == sub + (i % per_lanes) * TILE
                for j in range(TILE):
                    picked = jnp.where(here, row["g", v, j], 0.0)
                    col[i, j] = jnp.broadcast_to(jnp.sum(picked, axis=1, keepdims=True), shape)
        for j in range(TILE):
            scale = lax.rsqrt(a[j, j])
            for m in range(j + 1, TILE):
                a[j, m] = a[j, m] * scale
            for m in range(j + 1, TILE):
                for p in range(m, TILE):
                    a[m, p] = a[m, p] - a[j, m] * a[j, p]
            for i in range(k + 1, last):
                col[i, j] = col[i, j] * scale
                for m in range(j + 1, TILE):
                    col[i, m] = col[i, m] - a[j, m] * col[i, j]
            for kind, v in items:
                row[kind, v, j] = row[kind, v, j] * scale
                for m in range(j + 1, TILE):
                    row[kind, v, m] = row[kind, v, m] - a[j, m] * row[kind, v, j]
        for i in range(k + 1, last):
            for kind, v in items:
                ref = work if kind == "g" else inverse
                change = [col[i, j] * row[kind, v, j] for j in range(TILE)]
                while len(change) > 1:
                    change = [p + q for p, q in zip(change[::2], change[1::2])]
                ref[band(i), lanes(v)] = ref[band(i), lanes(v)] - change[0]
        for kind, v in items:
            tile = row[kind, v, TILE - 1]
            for j in range(TILE - 2, -1, -1):
                tile = jnp.where(sub == j, row[kind, v, j], tile)
            if kind == "g":
                if v == t:
                    tile = jnp.where(lane >= sub + base, tile, 0.0)
                tri_ref[band(k), lanes(v)] = tile
            else:
                inverse[band(k), lanes(v)] = tile

        if (k + 1) % group == 0:
            if pending is not None:
                at, low, span, drop, fill = pending
                work[at:, low:] = work[at:, low:] - drop
                inverse[at:, :span] = inverse[at:, :span] - fill
                pending = None
            at = (s + 2) * group * TILE
            if at < width:
                done = slice(s * group * TILE, (s + 1) * group * TILE)
                first = (at // LANES) * LANES
                low = first
                span = (t + 1) * LANES
                rest = tri_ref[done, :]
                top = pieces(rest)
                side = pieces(inverse[done, :span])
                left = jnp.concatenate([top[p][:, first:] for p, q in TERMS], axis=0)
                right = jnp.concatenate([top[q][:, low:] for p, q in TERMS], axis=0)
                dims = (((0,), (0,)), ((), ()))
                drop = lax.dot_general(left, right, dims, preferred_element_type=f32)
                right = jnp.concatenate([side[q] for p, q in TERMS], axis=0)
                fill = lax.dot_general(left, right, dims, preferred_element_type=f32)
                pending = at, low, span, drop[at - first:], fill[at - first:]
        if (k + 1) * TILE == LOW:
            fillers.append(pass_right)
            fillers += [functools.partial(finish_pass, c, chunk) for c in range(rows // chunk)]
        if (k + 1) * TILE == LANES:
            fillers.append(functools.partial(basis_right, 0))
            fillers += [functools.partial(finish_basis, c, 0, chunk) for c in range(rows // chunk)]
        if fillers:
            fillers.pop(0)()
    fillers.append(functools.partial(basis_right, 1))
    for c in range(rows // tail):
        fillers.append(functools.partial(finish_basis, c, 1, tail))
    for filler in fillers:
        filler()


def factor_call(gram, high, middle, low, group=2, chunk=256, tail=256):
    rows, width = high.shape
    f32 = jnp.float32
    vmem = pl.BlockSpec(memory_space=pltpu.VMEM)
    square = pltpu.VMEM((width, width), f32)
    return pl.pallas_call(
        functools.partial(factor_kernel, group, chunk, tail),
        out_shape=(
            jax.ShapeDtypeStruct((rows, width), f32),
            jax.ShapeDtypeStruct((width, width), f32),
            jax.ShapeDtypeStruct((rows, width), f32),
        ),
        in_specs=[vmem] * 4,
        out_specs=(vmem, vmem, vmem),
        scratch_shapes=[square, square, pltpu.VMEM((3, width, width), BF16)],
        compiler_params=pltpu.CompilerParams(vmem_limit_bytes=VMEM_LIMIT),
        name="factor",
    )(gram, high, middle, low)


def on_device(sizes, snapshots, live_rows, column_order):
    gram, *masked = masked_and_gram(snapshots, live_rows, column_order, sizes)
    return factor_call(gram, *masked)


def solution(mesh):
    placed = (P(("lon", "lat", "depth"), None), P(("lon", "lat", "depth")), P())
    sizes = (mesh.shape["lon"] // CORES, mesh.shape["lat"], mesh.shape["depth"])
    return jax.shard_map(
        functools.partial(on_device, sizes),
        mesh=mesh,
        in_specs=placed,
        out_specs=(P(("lon", "lat", "depth"), None), P(), P(("lon", "lat", "depth"), None)),
        check_vma=False,
    )
```

```python
import functools

import jax
import jax.numpy as jnp
from jax import lax
from jax.experimental import pallas as pl
from jax.experimental.pallas import tpu as pltpu
from jax.sharding import PartitionSpec as P

LOW = 32
CORES = 2
LANES = 128
TILE = 8
UNIT = 4
LOADS = 4
VMEM_LIMIT = 24 * 2**20
BF16 = jnp.bfloat16
TERMS = ((2, 0), (0, 2), (1, 1), (1, 0), (0, 1), (0, 0))
HIGHEST = lax.Precision.HIGHEST


def hops(d, n):
    return min(d % n, n - d % n)


def gram_kernel(total_rows, ny, nz, nx, snap_hbm, live_ref, order_hbm, out_ref, high_ref, middle_ref, low_ref,
                snap, order_ref, gram, from_plane, strip, from_z,
                load_sem, small_sem, line_sem, send_sem, recv_sem):
    rows, width = snap.shape
    lon = lax.axis_index("lon")
    core, y = lax.rem(lon, CORES), lax.div(lon, CORES)
    z, x = lax.axis_index("lat"), lax.axis_index("depth")
    f32 = jnp.float32
    data = (high_ref, middle_ref, low_ref)

    plane = [(dy, dx) for dy in range(ny) for dx in range(nx) if dy or dx]
    plane.sort(key=lambda d: -hops(d[0], ny) - hops(d[1], nx))
    line = sorted(range(1, nz), key=lambda d: -hops(d, nz))

    def other_core():
        return {"lon": y * CORES + 1 - core}

    def in_plane(dy, dx):
        return lax.rem(y + dy, ny), lax.rem(x + dx, nx)

    def at_plane(dy, dx):
        ty, tx = in_plane(dy, dx)
        return {"lon": ty * CORES + core, "depth": tx}

    def across(dy, dx):
        ty, tx = in_plane(dy, dx)
        return {"lon": ty * CORES + 1 - core, "depth": tx}

    def at_z(d):
        return {"lat": lax.rem(z + d, nz)}

    picks = pltpu.make_async_copy(order_hbm, order_ref, small_sem)
    picks.start()
    size = rows // LOADS
    loads = []
    for c in range(LOADS):
        here = pl.ds(c * size, size)
        load = pltpu.make_async_copy(snap_hbm.at[here], snap.at[here], load_sem.at[c])
        load.start()
        loads.append(load)

    reach = -(-nz // 4)
    near = [d for d in line if hops(d, nz) <= reach]
    ends = (reach, nz - reach)
    peers = [at_plane(*d) for d in plane] + [across(*d) for d in plane] + [at_z(d) for d in near] + [other_core()]
    barrier = pltpu.get_barrier_semaphore()
    for peer in peers:
        pl.semaphore_signal(barrier, inc=1, device_id=peer, device_id_type=pl.DeviceIdType.MESH)

    picks.wait()
    select = (lax.broadcasted_iota(jnp.int32, (width, width), 0) == order_ref[...]).astype(BF16)
    for c in range(LOADS):
        loads[c].wait()
        here = slice(c * size, (c + 1) * size)
        live = lax.broadcasted_iota(jnp.int32, (size, width), 0) + c * size < live_ref[0]
        for piece, ref in zip(pieces(jnp.where(live, snap[here, :], 0.0)), data):
            ref[here, :] = jnp.dot(piece, select, preferred_element_type=f32).astype(BF16)
    def inner(a, b):
        return lax.dot_general(a, b, (((0,), (0,)), ((), ())), preferred_element_type=f32)

    high, middle, low = (ref[...] for ref in data)
    cross = inner(high, low) + inner(high, middle)
    whole = (inner(middle, middle) + (cross + cross.T) + inner(high, high)) * (1.0 / total_rows)

    blocks = (whole[:LANES, :LANES], whole[:LANES, LANES:], whole[LANES:, LANES:])
    per_block = LANES // UNIT
    for at, block in enumerate(blocks):
        gram[at * per_block:(at + 1) * per_block] = block.reshape(per_block, UNIT, LANES)

    pl.semaphore_wait(barrier, len(peers))
    for d in ends:
        pl.semaphore_signal(line_sem, inc=1, device_id=at_z(d), device_id_type=pl.DeviceIdType.MESH)

    used = [0]

    def send(src, dst, peer):
        k = used[0]
        used[0] += 1
        copy = pltpu.make_async_remote_copy(
            src_ref=src, dst_ref=dst, send_sem=send_sem.at[k], recv_sem=recv_sem.at[k],
            device_id=peer, device_id_type=pl.DeviceIdType.MESH,
        )
        copy.start()
        return copy

    places = ny * nx
    n_strip = strip.shape[0]
    place = y * nx + x

    me = core * places + place

    def part_of(c, p):
        return pl.ds((c * places + p) * n_strip, n_strip)

    copies = []
    for d in plane:
        ty, tx = in_plane(*d)
        there = ty * nx + tx
        copies.append(send(gram.at[part_of(core, there)], from_plane.at[me], at_plane(*d)))
        copies.append(send(gram.at[part_of(1 - core, there)], from_plane.at[me], across(*d)))
    copies.append(send(gram.at[part_of(1 - core, place)], from_plane.at[me], other_core()))
    from_plane[me] = gram[part_of(core, place)]
    for copy in copies:
        copy.wait()
    total = from_plane[0]
    for s in range(1, CORES * places):
        total = total + from_plane[s]
    strip[...] = total

    pl.semaphore_wait(line_sem, len(ends))
    copies = [send(strip, from_z.at[z], at_z(d)) for d in line]
    from_z[z] = strip[...]
    for copy in copies:
        copy.wait()
    total = from_z[0]
    for s in range(1, nz):
        total = total + from_z[s]

    def strip_of(p):
        return out_ref.at[pl.ds((core * places + p) * n_strip, n_strip)]

    out_ref[pl.ds((core * places + place) * n_strip, n_strip)] = total
    copies = []
    for d in plane:
        copies.append(send(strip_of(place), strip_of(place), at_plane(*d)))
        copies.append(send(strip_of(place), strip_of(place), across(*d)))
    copies.append(send(strip_of(place), strip_of(place), other_core()))
    for copy in copies:
        copy.wait()


def masked_and_gram(snapshots, live_rows, column_order, sizes):
    rows, width = snapshots.shape
    ny, nz, nx = sizes
    places = ny * nx
    units = 3 * LANES // UNIT
    n_strip = units // (CORES * places)
    copies = 2 * (CORES * places - 1) + (nz - 1)
    total_rows = rows * CORES * places * nz
    f32 = jnp.float32
    tile = (UNIT, LANES)

    def in_hbm(array):
        return pltpu.with_memory_space_constraint(array, pltpu.HBM)

    gram, *masked = pl.pallas_call(
        functools.partial(gram_kernel, total_rows, ny, nz, nx),
        out_shape=(
            jax.ShapeDtypeStruct((units, *tile), f32),
            *[jax.ShapeDtypeStruct((rows, width), BF16)] * 3,
        ),
        in_specs=[
            pl.BlockSpec(memory_space=pltpu.HBM),
            pl.BlockSpec(memory_space=pltpu.SMEM),
            pl.BlockSpec(memory_space=pltpu.HBM),
        ],
        out_specs=(pl.BlockSpec(memory_space=pltpu.VMEM),) * 4,
        scratch_shapes=[
            pltpu.VMEM((rows, width), f32),
            pltpu.VMEM((1, width), jnp.int32),
            pltpu.VMEM((units, *tile), f32),
            pltpu.VMEM((CORES * places, n_strip, *tile), f32),
            pltpu.VMEM((n_strip, *tile), f32),
            pltpu.VMEM((nz, n_strip, *tile), f32),
            pltpu.SemaphoreType.DMA((LOADS,)),
            pltpu.SemaphoreType.DMA,
            pltpu.SemaphoreType.REGULAR,
            pltpu.SemaphoreType.DMA((copies,)),
            pltpu.SemaphoreType.DMA((copies,)),
        ],
        compiler_params=pltpu.CompilerParams(collective_id=0, has_side_effects=True, vmem_limit_bytes=VMEM_LIMIT),
        name="gram_allreduce",
    )(in_hbm(snapshots), live_rows, in_hbm(column_order.reshape(1, width)))
    return gram.reshape(3 * LANES, LANES), *masked


def pieces(value):
    high = value.astype(BF16)
    rest = value - high.astype(jnp.float32)
    middle = rest.astype(BF16)
    return high, middle, (rest - middle.astype(jnp.float32)).astype(BF16)


def product(a, b, dims):
    out = None
    for p, q in TERMS:
        term = lax.dot_general(a[p], b[q], (dims, ((), ())), preferred_element_type=jnp.float32)
        out = term if out is None else out + term
    return out


def factor_kernel(group, chunk, tail, gram_ref, high_ref, middle_ref, low_ref, basis_ref, tri_ref, pass_ref, work, inverse, right_ref):
    rows, width = high_ref.shape
    blocks = width // TILE
    per_lanes = LANES // TILE
    f32 = jnp.float32
    shape = (TILE, LANES)
    sub = lax.broadcasted_iota(jnp.int32, shape, 0)
    lane = lax.broadcasted_iota(jnp.int32, shape, 1)
    data = (high_ref, middle_ref, low_ref)

    def band(i):
        return slice(i * TILE, (i + 1) * TILE)

    def lanes(v):
        return slice(v * LANES, (v + 1) * LANES)

    work[:LANES, :LANES] = gram_ref[:LANES, :]
    work[:LANES, LANES:] = gram_ref[LANES:2 * LANES, :]
    work[LANES:, :LANES] = jnp.zeros((width - LANES, LANES), f32)
    work[LANES:, LANES:] = gram_ref[2 * LANES:, :]
    row_id = lax.broadcasted_iota(jnp.int32, (width, width), 0)
    col_id = lax.broadcasted_iota(jnp.int32, (width, width), 1)
    identity = (row_id == col_id).astype(f32)
    inverse[...] = identity
    tri_ref[...] = jnp.zeros_like(tri_ref)
    right_ref[0] = identity.astype(BF16)
    right_ref[1] = jnp.zeros((width, width), BF16)
    right_ref[2] = jnp.zeros((width, width), BF16)

    def pass_right():
        left = pieces(inverse[:LOW, :LOW])
        right = pieces(tri_ref[:LOW, :])
        left = jnp.concatenate([left[p] for p, q in TERMS], axis=0)
        right = jnp.concatenate([right[q] for p, q in TERMS], axis=0)
        taken = lax.dot_general(left, right, (((0,), (0,)), ((), ())), preferred_element_type=f32)
        for p, piece in enumerate(pieces(identity[:LOW] - taken)):
            right_ref[p, :LOW, :] = piece

    def finish_pass(c, size):
        here = slice(c * size, (c + 1) * size)
        right = [right_ref[p] for p in range(3)]
        pass_ref[here, :] = product([ref[here, :] for ref in data], right, ((1,), (0,)))

    def finish_basis(c, half, size):
        here = slice(c * size, (c + 1) * size)
        depth = (half + 1) * LANES
        right = [right_ref[p, :LANES, :depth] for p in range(3)]
        basis_ref[here, lanes(half)] = product([ref[here, :depth] for ref in data], right, ((1,), (1,)))

    def basis_right(half):
        depth = (half + 1) * LANES
        for p, piece in enumerate(pieces(inverse[lanes(half), :depth])):
            right_ref[p, :LANES, :depth] = piece

    fillers = []
    pending = None

    for k in range(blocks):
        t = k // per_lanes
        base = (k % per_lanes) * TILE
        s = k // group
        last = min((s + 2) * group, blocks)
        row = {}
        for j in range(TILE):
            r = k * TILE + j
            for v in range(t, width // LANES):
                row["g", v, j] = jnp.broadcast_to(work[r:r + 1, lanes(v)], shape)
            for v in range(0, t + 1):
                row["x", v, j] = jnp.broadcast_to(inverse[r:r + 1, lanes(v)], shape)
        items = [("g", v) for v in range(t, width // LANES)] + [("x", v) for v in range(0, t + 1)]
        a = {}
        for j in range(TILE):
            for m in range(j, TILE):
                a[j, m] = jnp.broadcast_to(row["g", t, j][:, base + m:base + m + 1], shape)
        col = {}
        for i in range(k + 1, last):
            v = i // per_lanes
            if i < (s + 1) * group:
                tile = work[band(i), lanes(v)]
                for j in range(TILE):
                    col[i, j] = jnp.broadcast_to(tile[:, base + j:base + j + 1], shape)
            else:
                here = lane == sub + (i % per_lanes) * TILE
                for j in range(TILE):
                    picked = jnp.where(here, row["g", v, j], 0.0)
                    col[i, j] = jnp.broadcast_to(jnp.sum(picked, axis=1, keepdims=True), shape)
        for j in range(TILE):
            scale = lax.rsqrt(a[j, j])
            for m in range(j + 1, TILE):
                a[j, m] = a[j, m] * scale
            for m in range(j + 1, TILE):
                for p in range(m, TILE):
                    a[m, p] = a[m, p] - a[j, m] * a[j, p]
            for i in range(k + 1, last):
                col[i, j] = col[i, j] * scale
                for m in range(j + 1, TILE):
                    col[i, m] = col[i, m] - a[j, m] * col[i, j]
            for kind, v in items:
                row[kind, v, j] = row[kind, v, j] * scale
                for m in range(j + 1, TILE):
                    row[kind, v, m] = row[kind, v, m] - a[j, m] * row[kind, v, j]
        for i in range(k + 1, last):
            for kind, v in items:
                ref = work if kind == "g" else inverse
                change = [col[i, j] * row[kind, v, j] for j in range(TILE)]
                while len(change) > 1:
                    change = [p + q for p, q in zip(change[::2], change[1::2])]
                ref[band(i), lanes(v)] = ref[band(i), lanes(v)] - change[0]
        for kind, v in items:
            tile = row[kind, v, TILE - 1]
            for j in range(TILE - 2, -1, -1):
                tile = jnp.where(sub == j, row[kind, v, j], tile)
            if kind == "g":
                if v == t:
                    tile = jnp.where(lane >= sub + base, tile, 0.0)
                tri_ref[band(k), lanes(v)] = tile
            else:
                inverse[band(k), lanes(v)] = tile

        if (k + 1) % group == 0:
            if pending is not None:
                at, low, span, drop, fill = pending
                work[at:, low:] = work[at:, low:] - drop
                inverse[at:, :span] = inverse[at:, :span] - fill
                pending = None
            at = (s + 2) * group * TILE
            if at < width:
                done = slice(s * group * TILE, (s + 1) * group * TILE)
                first = (at // LANES) * LANES
                low = first
                span = (t + 1) * LANES
                rest = tri_ref[done, :]
                top = pieces(rest)
                side = pieces(inverse[done, :span])
                left = jnp.concatenate([top[p][:, first:] for p, q in TERMS], axis=0)
                right = jnp.concatenate([top[q][:, low:] for p, q in TERMS], axis=0)
                dims = (((0,), (0,)), ((), ()))
                drop = lax.dot_general(left, right, dims, preferred_element_type=f32)
                right = jnp.concatenate([side[q] for p, q in TERMS], axis=0)
                fill = lax.dot_general(left, right, dims, preferred_element_type=f32)
                pending = at, low, span, drop[at - first:], fill[at - first:]
        if (k + 1) * TILE == LOW:
            fillers.append(pass_right)
            fillers += [functools.partial(finish_pass, c, chunk) for c in range(rows // chunk)]
        if (k + 1) * TILE == LANES:
            fillers.append(functools.partial(basis_right, 0))
            fillers += [functools.partial(finish_basis, c, 0, chunk) for c in range(rows // chunk)]
        if fillers:
            fillers.pop(0)()
    fillers.append(functools.partial(basis_right, 1))
    for c in range(rows // tail):
        fillers.append(functools.partial(finish_basis, c, 1, tail))
    for filler in fillers:
        filler()


def factor_call(gram, high, middle, low, group=2, chunk=256, tail=256):
    rows, width = high.shape
    f32 = jnp.float32
    vmem = pl.BlockSpec(memory_space=pltpu.VMEM)
    square = pltpu.VMEM((width, width), f32)
    return pl.pallas_call(
        functools.partial(factor_kernel, group, chunk, tail),
        out_shape=(
            jax.ShapeDtypeStruct((rows, width), f32),
            jax.ShapeDtypeStruct((width, width), f32),
            jax.ShapeDtypeStruct((rows, width), f32),
        ),
        in_specs=[vmem] * 4,
        out_specs=(vmem, vmem, vmem),
        scratch_shapes=[square, square, pltpu.VMEM((3, width, width), BF16)],
        compiler_params=pltpu.CompilerParams(vmem_limit_bytes=VMEM_LIMIT),
        name="factor",
    )(gram, high, middle, low)


def on_device(sizes, snapshots, live_rows, column_order):
    gram, *masked = masked_and_gram(snapshots, live_rows, column_order, sizes)
    return factor_call(gram, *masked)


def solution(mesh):
    placed = (P(("lon", "lat", "depth"), None), P(("lon", "lat", "depth")), P())
    sizes = (mesh.shape["lon"] // CORES, mesh.shape["lat"], mesh.shape["depth"])
    return jax.shard_map(
        functools.partial(on_device, sizes),
        mesh=mesh,
        in_specs=placed,
        out_specs=(P(("lon", "lat", "depth"), None), P(), P(("lon", "lat", "depth"), None)),
        check_vma=False,
    )
```
